256 devices in a mesh: frow: 8 (over z_lo, core), fcol: 32 (over x, z_hi, y).
Axes of the slice: x: 4, y: 4, z: 8 (z_hi: 2, z_lo: 4; z = z_hi * 4 + z_lo), core: 2. Of those that a mesh axis runs over, the one named last changes fastest.
Arguments:
- right_side: float32 [64, 1024, 256], P('frow', 'fcol'), may hold values from -6 to 6
- noise_weight: float32 [64, 1024, 256], P('frow', 'fcol'), may hold values from 3 to 4.5
- stencils: bfloat16 [9, 256, 256], replicated, may hold values from -1 to 1, as said below
- neighbours: int32 [64, 1024, 9], P('frow', 'fcol'), may hold values from -1 to 65535, as said below
Outputs:
- solution: float32 [64, 1024, 256], P('frow', 'fcol')
- coarse_residual: float32 [32, 512, 256], P('frow')
The draws below stay inside these ranges and needn't reach their ends.
Inputs may be any that keep to these rules, and one draw needn't show every extreme that they name: `neighbours`: each entry is -1 (an empty slot) or the index r * 1024 + c of the tile at row r = own row + k // 3 - 1 and column c = own column + k % 3 - 1 for slot k; slot 4 always holds the tile itself; if tile t holds tile s in slot k, then s holds t in slot 8 - k. stencils[8 - k] is the transpose of stencils[k], and stencils[4] is symmetric.
All inputs are finite; a program needn't handle non-finite values.
Results may differ from the reference program's by a relative error of at most 0.0031.
Values may be sent and summed in bfloat16 or wider, within the bound.
A program may use at most 64 MiB of HBM per device.

```python
import math
import jax
import jax.numpy as jnp
from jax import lax

PIX = 256
STENCILS = 9
DEG = 3
GRID_ROWS = 64
GRID_COLS = 1024


def draw_neighbours(key, part):
    shape_three = (GRID_ROWS, GRID_COLS, STENCILS)
    tile_row = lax.broadcasted_iota(jnp.int32, shape_three, 0)
    tile_col = lax.broadcasted_iota(jnp.int32, shape_three, 1)
    slot_index = lax.broadcasted_iota(jnp.int32, shape_three, 2)
    base_drop = jax.random.randint(jax.random.fold_in(key, 17), shape_three, 0, 16) == 0
    near_row = tile_row + slot_index // 3 - 1
    near_col = tile_col + slot_index % 3 - 1
    inside = (near_row >= 0) & (near_row < GRID_ROWS) & (near_col >= 0) & (near_col < GRID_COLS)
    clamp_row = jnp.clip(near_row, 0, GRID_ROWS - 1)
    clamp_col = jnp.clip(near_col, 0, GRID_COLS - 1)
    mirror_index = ((clamp_row * GRID_COLS + clamp_col) * STENCILS + (8 - slot_index)).astype(jnp.int32)
    mirrored = jnp.take(base_drop.reshape(-1), mirror_index.reshape(-1), axis=0).reshape(shape_three)
    dropped = jnp.where(slot_index < 4, base_drop, jnp.where(slot_index > 4, mirrored, False))
    keep = inside & jnp.logical_not(dropped)
    return jnp.where(keep, near_row * GRID_COLS + near_col, -1).astype(jnp.int32)


def draw_stencils(key, part):
    first_key, second_key = jax.random.split(jax.random.fold_in(key, 29))
    scale = (16.0 * PIX) ** (-0.5)
    lower_blocks = jnp.clip(jax.random.normal(first_key, (4, PIX, PIX), jnp.float32), -6.0, 6.0) * scale
    square = jax.random.normal(second_key, (PIX, PIX), jnp.float32)
    middle = jnp.clip((square + square.T) * 0.5 ** 0.5, -6.0, 6.0) * scale
    lower_blocks = lower_blocks.astype(jnp.bfloat16)
    middle = middle.astype(jnp.bfloat16)
    upper_blocks = jnp.transpose(lower_blocks[::-1], (0, 2, 1))
    return jnp.concatenate([lower_blocks, middle[None], upper_blocks], 0)


def shard_levels(rng, extent, cuts, low, top_value):
    factor_of = 1.0
    for position, blocks in cuts:
        draws = jax.random.uniform(jax.random.fold_in(jax.random.fold_in(rng, 6), position), (blocks,), jnp.float32, low / len(cuts), top_value / len(cuts))
        factor_of = factor_of * jnp.repeat(jnp.exp(draws), extent[position] // blocks).reshape((-1,) + (1,) * (len(extent) - 1 - position))
    return factor_of


def centred(key, dims, deviation, bound, cuts=(), dtype=jnp.bfloat16):
    values = jax.random.normal(key, dims, jnp.float32) * deviation
    if len(cuts) > 0:
        values = shard_levels(key, dims, cuts, -0.22, 0.18) * values
    return jnp.clip(values, min=-bound, max=bound).astype(dtype)


def setup_inputs(seed: int = 0) -> dict:
    keys = jax.random.split(jax.random.key(seed), 5)
    right_side = centred(keys[0], (GRID_ROWS, GRID_COLS, PIX), 1.0, 6.0, ((0, 8), (1, 32)), jnp.float32)
    noise_weight = jnp.clip(jnp.exp(math.log(4.5) - 0.4054651 * jax.random.uniform(keys[1], (GRID_ROWS, GRID_COLS, PIX), jnp.float32) ** shard_levels(keys[1], (GRID_ROWS, GRID_COLS, PIX), ((0, 8), (1, 32)), -0.2, 0.2)), 3.0, 4.5)
    stencils = draw_stencils(jax.random.fold_in(keys[4], 71), 0)
    neighbours = draw_neighbours(jax.random.fold_in(keys[4], 71), 0)
    return {"right_side": right_side, "noise_weight": noise_weight, "stencils": stencils, "neighbours": neighbours}


lower_edge = 1.5
upper_edge = 6.0


def restrict(paired_block):
    height, width, doubled = paired_block.shape
    pixels = doubled // 2
    summed = jnp.sum(paired_block.reshape(height // 2, 2, width, 2, pixels // 4, 4), axis=5)
    return jnp.transpose(summed, (0, 2, 1, 3, 4)).reshape(height // 2, width, pixels)


def smooth(right_side, operate):
    center = 0.5 * (upper_edge + lower_edge)
    half_width = 0.5 * (upper_edge - lower_edge)
    spread_ratio = center / half_width
    solution = jnp.zeros_like(right_side)
    residual = right_side
    for sweep_index in range(2):
        ratio_now = 1.0 / spread_ratio
        direction = residual / center
        for step_index in range(DEG):
            solution = solution + direction
            residual = residual - operate(direction)
            if step_index < DEG - 1:
                ratio_next = 1.0 / (2.0 * spread_ratio - ratio_now)
                direction = (ratio_next * ratio_now) * direction + (2.0 * ratio_next / half_width) * residual
                ratio_now = ratio_next
    return solution, residual


def reference(right_side, noise_weight, stencils, neighbours):
    tiles = GRID_ROWS * GRID_COLS
    stencil_matrix = stencils.reshape(STENCILS * PIX, PIX)
    targets = jnp.where(neighbours < 0, tiles, neighbours).astype(jnp.int32)

    def operate(direction):
        rounded = direction.astype(jnp.bfloat16)
        flattened = jnp.concatenate([rounded.reshape(tiles, PIX), jnp.zeros((1, PIX), jnp.bfloat16)], 0)

        def one_row(row_targets):
            picked = jnp.take(flattened, row_targets.reshape(-1), axis=0).reshape(GRID_COLS, STENCILS * PIX)
            return jnp.dot(picked, stencil_matrix, preferred_element_type=jnp.float32)

        coupled = lax.map(one_row, targets)
        return noise_weight * direction + coupled

    solution, residual = smooth(right_side, operate)
    coarse_residual = restrict(residual.reshape(GRID_ROWS, GRID_COLS // 2, 2 * PIX))
    return solution, coarse_residual
```

```python
import functools

import jax
import jax.numpy as jnp
from jax import lax
from jax.experimental import pallas as pl
from jax.experimental.pallas import tpu as pltpu
from jax.sharding import PartitionSpec as P

MESH = pl.DeviceIdType.MESH
LOWER, UPPER, DEG, SWEEPS = 1.5, 6.0, 3, 2
HALO = DEG * SWEEPS
SIDE = 8


def coefficients():
    center = 0.5 * (UPPER + LOWER)
    half_width = 0.5 * (UPPER - LOWER)
    spread = center / half_width
    steps = []
    for _ in range(SWEEPS):
        ratio = 1.0 / spread
        for step in range(DEG):
            if step < DEG - 1:
                after = 1.0 / (2.0 * spread - ratio)
                steps.append((after * ratio, 2.0 * after / half_width))
                ratio = after
            else:
                steps.append((0.0, 1.0 / center))
    return center, steps


def kernel(
    sizes, rs, nw, st, nb, sol_ref, out_ref, res, wgt, drc, dir_bf, msk, nbx, stv, fin, halo_send, halo_recv, loc_sem, g_send, g_recv
):
    n_row, n_col, rows, cols, pix, slots = sizes
    ext_rows, ext_cols = rows + 2 * HALO, cols + 2 * SIDE
    frow, fcol = lax.axis_index("frow"), lax.axis_index("fcol")

    def at(dr, dc):
        return (lax.rem(frow + (dr + n_row), n_row), lax.rem(fcol + (dc + n_col), n_col))

    local = [
        pltpu.make_async_copy(nb, nbx.at[4], loc_sem.at[0]),
        pltpu.make_async_copy(rs, res.at[pl.ds(HALO, rows), pl.ds(SIDE, cols)], loc_sem.at[1]),
        pltpu.make_async_copy(nw, wgt.at[pl.ds(HALO, rows), pl.ds(SIDE, cols)], loc_sem.at[2]),
        pltpu.make_async_copy(st, stv, loc_sem.at[3]),
    ]
    for copy in local:
        copy.start()

    barrier = pltpu.get_barrier_semaphore()
    for dr in (-1, 1):
        for dc in (-1, 0, 1):
            pl.semaphore_signal(barrier, inc=1, device_id=at(dr, dc), device_id_type=MESH)

    def hail(i, c):
        pl.semaphore_signal(barrier, inc=1, device_id=(frow, lax.rem(fcol + i, n_col)), device_id_type=MESH)
        return c

    lax.fori_loop(1, n_col, hail, 0)
    pl.semaphore_wait(barrier, 6 + n_col - 1)

    halo = {}
    for dr in (-1, 0, 1):
        for dc in (-1, 0, 1):
            if dr == 0 and dc == 0:
                continue
            src_r = {-1: pl.ds(0, HALO), 0: pl.ds(0, rows), 1: pl.ds(rows - HALO, HALO)}[dr]
            dst_r = {-1: pl.ds(HALO + rows, HALO), 0: pl.ds(HALO, rows), 1: pl.ds(0, HALO)}[dr]
            src_c = {-1: pl.ds(0, SIDE), 0: pl.ds(0, cols), 1: pl.ds(cols - SIDE, SIDE)}[dc]
            dst_c = {-1: pl.ds(SIDE + cols, SIDE), 0: pl.ds(SIDE, cols), 1: pl.ds(0, SIDE)}[dc]
            slot = (1 - dr) * 3 + (1 - dc)
            index = slot if slot < 4 else slot - 1
            trio = []
            for j, (src, dst) in enumerate(
                (
                    (nb, nbx.at[slot]),
                    (rs.at[src_r, src_c], res.at[dst_r, dst_c]),
                    (nw.at[src_r, src_c], wgt.at[dst_r, dst_c]),
                )
            ):
                copy = pltpu.make_async_remote_copy(
                    src_ref=src,
                    dst_ref=dst,
                    send_sem=halo_send.at[index * 3 + j],
                    recv_sem=halo_recv.at[index * 3 + j],
                    device_id=at(dr, dc),
                    device_id_type=MESH,
                )
                trio.append(copy)
            halo[dr, dc] = trio
    for key in ((0, 1), (0, -1), (1, 1), (1, -1), (-1, 1), (-1, -1), (1, 0), (-1, 0)):
        for copy in halo[key]:
            copy.start()
    for copy in local:
        copy.wait()
    for key in halo:
        for copy in halo[key]:
            copy.wait()

    for block, first, last, base in ((0, rows - HALO, rows, 0), (1, 0, rows, HALO), (2, 0, HALO, HALO + rows)):
        def turned(slot):
            flat = jnp.where(nbx[slot] >= 0, 1.0, 0.0).astype(jnp.float32).reshape(slots * rows, cols)
            return jnp.transpose(flat)

        whole = jnp.concatenate(
            [turned(3 * block)[cols - SIDE :], turned(3 * block + 1), turned(3 * block + 2)[:SIDE]], axis=0
        )
        for k in range(slots):
            for row in range(first, last):
                m = k * rows + row
                wide = jnp.broadcast_to(whole[:, m : m + 1], (ext_cols, 128)).astype(jnp.bfloat16)
                msk[k, pl.ds((base + row - first) * ext_cols, ext_cols), :] = wide

    center, steps = coefficients()

    def put(buf, t0, count, value):
        for j, shift in enumerate((1, 0, count - 1)):
            moved = value if shift == 0 else pltpu.roll(value, shift, axis=0)
            dir_bf[buf, j, pl.ds(t0, count), :] = moved.astype(jnp.bfloat16)

    res_flat = res.reshape(ext_rows * ext_cols, pix)
    wgt_flat = wgt.reshape(ext_rows * ext_cols, pix)

    def begin(i, c):
        t0 = pl.multiple_of(i * (2 * ext_cols), 2 * ext_cols)
        d = res_flat[pl.ds(t0, 2 * ext_cols), :] * (1.0 / center)
        drc[pl.ds(t0, 2 * ext_cols), :] = d
        put(0, t0, 2 * ext_cols, d)
        return c

    lax.fori_loop(0, ext_rows // 2, begin, 0)

    drc_cube = drc.reshape(ext_rows, ext_cols, pix)

    for op in range(HALO):
        now, later = op % 2, (op + 1) % 2
        low = op + 1
        count = ext_rows - 2 * low
        chunk = CHUNK[op]
        size = chunk * ext_cols
        own = drc_cube[pl.ds(HALO, rows), pl.ds(SIDE, cols), :]
        sol_ref[...] = own if op == 0 else sol_ref[...] + own

        def apply(i, c, now=now, later=later, low=low, size=size, op=op):
            t0 = pl.multiple_of(low * ext_cols + i * size, ext_cols)
            parts = []
            for k in range(slots):
                src = t0 + (k // 3 - 1) * ext_cols
                part = dir_bf[now, k % 3, pl.ds(pl.multiple_of(src, ext_cols), size), :]
                keep = msk[k, pl.ds(t0, size), :]
                parts.append(part * jnp.concatenate([keep, keep], axis=1))
            coupled = jnp.dot(
                jnp.concatenate(parts, axis=1), stv[...].reshape(slots * pix, pix), preferred_element_type=jnp.float32
            )
            d = drc[pl.ds(t0, size), :]
            r = res_flat[pl.ds(t0, size), :] - (wgt_flat[pl.ds(t0, size), :] * d + coupled)
            if op == HALO - 1:
                for h in range(pix // 128):
                    fin[h] = r[:, h * 128 : (h + 1) * 128]
            else:
                res_flat[pl.ds(t0, size), :] = r
                old, new = steps[op]
                d = new * r if old == 0.0 else old * d + new * r
                drc[pl.ds(t0, size), :] = d
                put(later, t0, size, d)
            return c

        trips = count // chunk
        if trips == 1:
            apply(0, 0)
        else:
            lax.fori_loop(0, trips, apply, 0)

    pixel = lax.broadcasted_iota(jnp.int32, (pix, 128), 0)
    lane = lax.broadcasted_iota(jnp.int32, (pix, 128), 1)
    fold = jnp.where(pixel // 4 == lane % 64, 1.0, 0.0).astype(jnp.bfloat16)
    pieces = []
    for a in range(2):
        for b in range(2):
            for R in range(rows // 2):
                begin_at = (2 * R + a) * ext_cols + SIDE + b
                pieces.append(
                    jnp.concatenate(
                        [fin[h, pl.ds(begin_at, cols // 2, stride=2), :] for h in range(pix // 128)], axis=1
                    )
                )
    stack = jnp.concatenate(pieces, axis=0)
    high = stack.astype(jnp.bfloat16)
    low_part = (stack - high.astype(jnp.float32)).astype(jnp.bfloat16)
    summed = jnp.dot(high, fold, preferred_element_type=jnp.float32) + jnp.dot(
        low_part, fold, preferred_element_type=jnp.float32
    )
    quarter = (rows // 2) * (cols // 2)
    y = [summed[q * quarter : (q + 1) * quarter] for q in range(4)]
    left = lax.broadcasted_iota(jnp.int32, (quarter, 128), 1) < 64
    coarse = jnp.concatenate([jnp.where(left, y[0], y[1]), jnp.where(left, y[2], y[3])], axis=1).astype(jnp.bfloat16)
    mine = pl.ds(pl.multiple_of(fcol * (cols // 2), cols // 2), cols // 2)
    out_ref[:, mine, :] = coarse.reshape(rows // 2, cols // 2, pix)

    def given(i):
        return pltpu.make_async_remote_copy(
            src_ref=out_ref.at[:, mine, :],
            dst_ref=out_ref.at[:, mine, :],
            send_sem=g_send.at[i],
            recv_sem=g_recv.at[i],
            device_id=(frow, lax.rem(fcol + i, n_col)),
            device_id_type=MESH,
        )

    def start(i, c):
        given(i).start()
        return c

    def finish(i, c):
        other = lax.rem(fcol - i + n_col, n_col)
        theirs = pl.ds(pl.multiple_of(other * (cols // 2), cols // 2), cols // 2)
        pltpu.make_async_remote_copy(
            src_ref=out_ref.at[:, theirs, :],
            dst_ref=out_ref.at[:, theirs, :],
            send_sem=g_send.at[i],
            recv_sem=g_recv.at[i],
            device_id=(frow, lax.rem(fcol + i, n_col)),
            device_id_type=MESH,
        ).wait_recv()
        given(i).wait_send()
        return c

    lax.fori_loop(1, n_col, start, 0)
    lax.fori_loop(1, n_col, finish, 0)


CHUNK = (9, 8, 7, 6, 5, 8)


def solution(mesh):
    n_row, n_col = mesh.shape["frow"], mesh.shape["fcol"]

    def body(right_side, noise_weight, stencils, neighbours):
        rows, cols, pix = right_side.shape
        slots = stencils.shape[0]
        ext = (rows + 2 * HALO, cols + 2 * SIDE)
        tiles = ext[0] * ext[1]
        listed = jnp.transpose(neighbours, (2, 0, 1))
        smooth, coarse = pl.pallas_call(
            functools.partial(kernel, (n_row, n_col, rows, cols, pix, slots)),
            out_shape=(
                jax.ShapeDtypeStruct((rows, cols, pix), jnp.float32),
                jax.ShapeDtypeStruct((rows // 2, cols // 2 * n_col, pix), jnp.bfloat16),
            ),
            in_specs=[pl.BlockSpec(memory_space=pl.ANY)] * 4,
            out_specs=(pl.BlockSpec(memory_space=pltpu.VMEM), pl.BlockSpec(memory_space=pltpu.VMEM)),
            scratch_shapes=[
                pltpu.VMEM(ext + (pix,), jnp.float32),
                pltpu.VMEM(ext + (pix,), jnp.float32),
                pltpu.VMEM((tiles, pix), jnp.float32),
                pltpu.VMEM((2, 3, tiles, pix), jnp.bfloat16),
                pltpu.VMEM((slots, tiles, 128), jnp.bfloat16),
                pltpu.VMEM((9, slots, rows, cols), jnp.int32),
                pltpu.VMEM((slots, pix, pix), jnp.bfloat16),
                pltpu.VMEM((pix // 128, rows * ext[1], 128), jnp.float32),
                pltpu.SemaphoreType.DMA((24,)),
                pltpu.SemaphoreType.DMA((24,)),
                pltpu.SemaphoreType.DMA((4,)),
                pltpu.SemaphoreType.DMA((n_col,)),
                pltpu.SemaphoreType.DMA((n_col,)),
            ],
            compiler_params=pltpu.CompilerParams(
                collective_id=0, has_side_effects=True, vmem_limit_bytes=48 << 20
            ),
        )(right_side, noise_weight, stencils, listed)
        return smooth, coarse.astype(jnp.float32)

    placed = (P("frow", "fcol", None), P("frow", "fcol", None), P(), P("frow", "fcol", None))
    return jax.shard_map(
        body,
        mesh=mesh,
        in_specs=placed,
        out_specs=(P("frow", "fcol", None), P("frow", None, None)),
        check_vma=False,
    )
```

```python
import functools

import jax
import jax.numpy as jnp
from jax import lax
from jax.experimental import pallas as pl
from jax.experimental.pallas import tpu as pltpu
from jax.sharding import PartitionSpec as P

MESH = pl.DeviceIdType.MESH
LOWER, UPPER, DEG, SWEEPS = 1.5, 6.0, 3, 2
HALO = DEG * SWEEPS
SIDE = 8
MIDDLE = 3.75


def coefficients():
    center = 0.5 * (UPPER + LOWER)
    half_width = 0.5 * (UPPER - LOWER)
    spread = center / half_width
    steps = []
    for _ in range(SWEEPS):
        ratio = 1.0 / spread
        for step in range(DEG):
            if step < DEG - 1:
                after = 1.0 / (2.0 * spread - ratio)
                steps.append((after * ratio, 2.0 * after / half_width))
                ratio = after
            else:
                steps.append((0.0, 1.0 / center))
    return center, steps


def kernel(
    sizes, rs, nw, st, nb, sol_ref, out_ref, res, wgt, drc, dir_bf, msk, fin, own_nb, stv,
    band_out, band_in, strip_out, strip_in, corner_in, loc_sem, h_send, h_recv, g_send, g_recv
):
    n_row, n_col, rows, cols, pix, slots = sizes
    ext_rows, ext_cols = rows + 2 * HALO, cols + 2 * SIDE
    frow, fcol = lax.axis_index("frow"), lax.axis_index("fcol")
    f32, bf16 = jnp.float32, jnp.bfloat16
    has = {"up": frow > 0, "down": frow < n_row - 1, "left": fcol > 0, "right": fcol < n_col - 1}
    beside = {"up": (frow - 1, fcol), "down": (frow + 1, fcol), "left": (frow, fcol - 1), "right": (frow, fcol + 1)}
    sides = ("up", "down", "left", "right")
    y, zh = lax.rem(fcol, 4), lax.rem(fcol // 4, 2)

    def along_x(d):
        return lax.rem(fcol + 8 * d, n_col)

    def along_y(d):
        return fcol - y + lax.rem(y + d, 4)

    partner = fcol + 4 - 8 * zh

    barrier = pltpu.get_barrier_semaphore()
    for side in sides:

        @pl.when(has[side])
        def _(side=side):
            pl.semaphore_signal(barrier, inc=1, device_id=beside[side], device_id_type=MESH)

    for peer in [along_x(d) for d in (1, 2, 3)] + [along_y(d) for d in (1, 2, 3)] + [partner]:
        pl.semaphore_signal(barrier, inc=1, device_id=(frow, peer), device_id_type=MESH)

    local = [
        pltpu.make_async_copy(nb, own_nb, loc_sem.at[0]),
        pltpu.make_async_copy(rs, res.at[pl.ds(HALO, rows), pl.ds(SIDE, cols)], loc_sem.at[1]),
        pltpu.make_async_copy(nw, wgt.at[pl.ds(HALO, rows), pl.ds(SIDE, cols)], loc_sem.at[2]),
        pltpu.make_async_copy(st, stv, loc_sem.at[3]),
    ]
    for copy in local:
        copy.start()

    for n, side in enumerate(("up", "down")):

        @pl.when(jnp.logical_not(has[side]))
        def _(n=n):
            band_in[n] = jnp.zeros(band_in.shape[1:], bf16)
            corner_in[2 * n] = jnp.zeros(corner_in.shape[1:], bf16)
            corner_in[2 * n + 1] = jnp.zeros(corner_in.shape[1:], bf16)

    for n, side in enumerate(("left", "right")):

        @pl.when(jnp.logical_not(has[side]))
        def _(n=n):
            strip_in[n] = jnp.zeros(strip_in.shape[1:], bf16)

    for copy in local[:3]:
        copy.wait()
    flat = jnp.where(own_nb[...] >= 0, 1.0, 0.0).astype(f32).reshape(slots * rows, cols)
    flat = jnp.concatenate([flat, jnp.zeros((128 - slots * rows, cols), f32)], axis=0)
    turned = jnp.transpose(flat)
    listed = jnp.concatenate([turned, jnp.zeros((cols, pix - 128), f32)], axis=1)
    half = rows // 2 - 1
    unit, small = 2 * cols, 2 * SIDE

    def spot(row, size, middle):
        return row * size + (middle if row >= half else 0)

    band_out[pl.ds(half * unit, cols), :] = listed.astype(bf16)
    for n, c0 in ((0, 0), (1, cols - SIDE)):
        strip_out[n, pl.ds(half * small, small), :] = jnp.concatenate(
            [listed[c0 : c0 + SIDE], jnp.zeros((SIDE, pix), f32)], axis=0
        ).astype(bf16)
    for row in range(rows):
        r = res[HALO + row, pl.ds(SIDE, cols), :]
        w = wgt[HALO + row, pl.ds(SIDE, cols), :] - MIDDLE
        band_out[pl.ds(spot(row, unit, cols), unit), :] = jnp.concatenate([r, w], axis=0).astype(bf16)
        for n, c0 in ((0, 0), (1, cols - SIDE)):
            strip_out[n, pl.ds(spot(row, small, small), small), :] = jnp.concatenate(
                [r[c0 : c0 + SIDE], w[c0 : c0 + SIDE]], axis=0
            ).astype(bf16)

    band_size = HALO * unit + cols
    corner_size = HALO * small + small

    def remote(src, dst, index, peer):
        return pltpu.make_async_remote_copy(
            src_ref=src, dst_ref=dst, send_sem=h_send.at[index], recv_sem=h_recv.at[index],
            device_id=peer, device_id_type=MESH,
        )

    far_band, far_strip = pl.ds((rows - HALO) * unit, band_size), pl.ds((rows - HALO) * small, corner_size)
    near_band, near_strip = pl.ds(0, band_size), pl.ds(0, corner_size)
    strips = [
        ("right", "left", lambda: remote(strip_out.at[1], strip_in.at[0], 0, beside["right"])),
        ("left", "right", lambda: remote(strip_out.at[0], strip_in.at[1], 1, beside["left"])),
    ]
    bands = [
        ("down", "up", lambda: remote(band_out.at[far_band], band_in.at[0], 2, beside["down"])),
        ("up", "down", lambda: remote(band_out.at[near_band], band_in.at[1], 3, beside["up"])),
    ]
    corners = [
        [
            ("down", "up", lambda n=n: remote(strip_in.at[n, far_strip], corner_in.at[n], 4 + n, beside["down"])),
            ("up", "down", lambda n=n: remote(strip_in.at[n, near_strip], corner_in.at[2 + n], 6 + n, beside["up"])),
        ]
        for n in range(2)
    ]

    def each(copies, act, by):
        for entry in copies:

            @pl.when(has[entry[by]])
            def _(entry=entry):
                getattr(entry[2](), act)()

    amount = 7
    for side in sides:
        amount = amount + jnp.where(has[side], 1, 0)
    pl.semaphore_wait(barrier, amount)
    each(strips, "start", 0)
    each(bands, "start", 0)
    for n in range(2):
        each(strips[n : n + 1], "wait_recv", 1)
        each(corners[n], "start", 0)
    each(bands, "wait_recv", 1)
    for n in range(2):
        each(corners[n], "wait_recv", 1)

    for n, base in ((0, 0), (1, HALO + rows)):
        skip = (rows - HALO) if n == 0 else 0
        for i in range(HALO):
            row = i + skip
            o = spot(row, unit, cols) - skip * unit
            part = band_in[n, pl.ds(o, unit), :].astype(f32)
            res[base + i, pl.ds(SIDE, cols), :] = part[:cols]
            wgt[base + i, pl.ds(SIDE, cols), :] = part[cols:] + MIDDLE
            o = spot(row, small, small) - skip * small
            for m, c0 in ((0, 0), (1, SIDE + cols)):
                part = corner_in[2 * n + m, pl.ds(o, small), :].astype(f32)
                res[base + i, pl.ds(c0, SIDE), :] = part[:SIDE]
                wgt[base + i, pl.ds(c0, SIDE), :] = part[SIDE:] + MIDDLE
    for m, c0 in ((0, 0), (1, SIDE + cols)):
        for row in range(rows):
            part = strip_in[m, pl.ds(spot(row, small, small), small), :].astype(f32)
            res[HALO + row, pl.ds(c0, SIDE), :] = part[:SIDE]
            wgt[HALO + row, pl.ds(c0, SIDE), :] = part[SIDE:] + MIDDLE

    above, below = (half - rows + HALO), half
    for first, last, base, left, mid, right in (
        (
            rows - HALO, rows, 0,
            corner_in[0, pl.ds(above * small, small), :], band_in[0, pl.ds(above * unit, cols), :],
            corner_in[1, pl.ds(above * small, small), :],
        ),
        (
            0, rows, HALO,
            strip_in[0, pl.ds(half * small, small), :], None, strip_in[1, pl.ds(half * small, small), :],
        ),
        (
            0, HALO, HALO + rows,
            corner_in[2, pl.ds(below * small, small), :], band_in[1, pl.ds(below * unit, cols), :],
            corner_in[3, pl.ds(below * small, small), :],
        ),
    ):
        middle = turned if mid is None else mid.astype(f32)[:, :128]
        whole = jnp.concatenate([left.astype(f32)[:SIDE, :128], middle, right.astype(f32)[:SIDE, :128]], axis=0)
        for k in range(slots):
            for row in range(first, last):
                m = k * rows + row
                wide = jnp.broadcast_to(whole[:, m : m + 1], (ext_cols, 128)).astype(bf16)
                msk[k, pl.ds((base + row - first) * ext_cols, ext_cols), :] = wide
    local[3].wait()

    center, steps = coefficients()

    def put(buf, t0, count, value):
        for j, shift in enumerate((1, 0, count - 1)):
            moved = value if shift == 0 else pltpu.roll(value, shift, axis=0)
            dir_bf[buf, j, pl.ds(t0, count), :] = moved.astype(jnp.bfloat16)

    res_flat = res.reshape(ext_rows * ext_cols, pix)
    wgt_flat = wgt.reshape(ext_rows * ext_cols, pix)

    def begin(i, c):
        t0 = pl.multiple_of(i * (2 * ext_cols), 2 * ext_cols)
        d = res_flat[pl.ds(t0, 2 * ext_cols), :] * (1.0 / center)
        drc[pl.ds(t0, 2 * ext_cols), :] = d
        put(0, t0, 2 * ext_cols, d)
        return c

    lax.fori_loop(0, ext_rows // 2, begin, 0)

    drc_cube = drc.reshape(ext_rows, ext_cols, pix)

    for op in range(HALO):
        now, later = op % 2, (op + 1) % 2
        low = op + 1
        count = ext_rows - 2 * low
        chunk = CHUNK[op]
        size = chunk * ext_cols
        own = drc_cube[pl.ds(HALO, rows), pl.ds(SIDE, cols), :]
        sol_ref[...] = own if op == 0 else sol_ref[...] + own

        def apply(i, c, now=now, later=later, low=low, size=size, op=op):
            t0 = pl.multiple_of(low * ext_cols + i * size, ext_cols)
            parts = []
            for k in range(slots):
                src = t0 + (k // 3 - 1) * ext_cols
                part = dir_bf[now, k % 3, pl.ds(pl.multiple_of(src, ext_cols), size), :]
                keep = msk[k, pl.ds(t0, size), :]
                parts.append(part * jnp.concatenate([keep, keep], axis=1))
            coupled = jnp.dot(
                jnp.concatenate(parts, axis=1), stv[...].reshape(slots * pix, pix), preferred_element_type=jnp.float32
            )
            d = drc[pl.ds(t0, size), :]
            r = res_flat[pl.ds(t0, size), :] - (wgt_flat[pl.ds(t0, size), :] * d + coupled)
            if op == HALO - 1:
                for h in range(pix // 128):
                    fin[h] = r[:, h * 128 : (h + 1) * 128]
            else:
                res_flat[pl.ds(t0, size), :] = r
                old, new = steps[op]
                d = new * r if old == 0.0 else old * d + new * r
                drc[pl.ds(t0, size), :] = d
                put(later, t0, size, d)
            return c

        trips = count // chunk
        if trips == 1:
            apply(0, 0)
        else:
            lax.fori_loop(0, trips, apply, 0)

    pixel = lax.broadcasted_iota(jnp.int32, (pix, 128), 0)
    lane = lax.broadcasted_iota(jnp.int32, (pix, 128), 1)
    fold = jnp.where(pixel // 4 == lane % 64, 1.0, 0.0).astype(jnp.bfloat16)
    pieces = []
    for a in range(2):
        for b in range(2):
            for R in range(rows // 2):
                begin_at = (2 * R + a) * ext_cols + SIDE + b
                pieces.append(
                    jnp.concatenate(
                        [fin[h, pl.ds(begin_at, cols // 2, stride=2), :] for h in range(pix // 128)], axis=1
                    )
                )
    stack = jnp.concatenate(pieces, axis=0)
    high = stack.astype(jnp.bfloat16)
    low_part = (stack - high.astype(jnp.float32)).astype(jnp.bfloat16)
    summed = jnp.dot(high, fold, preferred_element_type=jnp.float32) + jnp.dot(
        low_part, fold, preferred_element_type=jnp.float32
    )
    quarter = (rows // 2) * (cols // 2)
    quads = [summed[q * quarter : (q + 1) * quarter] for q in range(4)]
    left = lax.broadcasted_iota(jnp.int32, (quarter, 128), 1) < 64
    coarse = jnp.concatenate([jnp.where(left, quads[0], quads[1]), jnp.where(left, quads[2], quads[3])], axis=1).astype(jnp.bfloat16)
    quarter_cols = cols // 2
    group = rows // 4

    def block(j, half=None):
        span = pl.ds(pl.multiple_of(j * quarter_cols, quarter_cols), quarter_cols)
        if half is None:
            return out_ref.at[:, span, :]
        return out_ref.at[pl.ds(half * group, group), span, :]

    out_ref[:, pl.ds(pl.multiple_of(fcol * quarter_cols, quarter_cols), quarter_cols), :] = coarse.reshape(
        rows // 2, quarter_cols, pix
    )

    def move(ref, index, peer):
        return pltpu.make_async_remote_copy(
            src_ref=ref, dst_ref=ref, send_sem=g_send.at[index], recv_sem=g_recv.at[index],
            device_id=(frow, peer), device_id_type=MESH,
        )

    routes = ((along_x, along_y), (along_y, along_x))

    def source(way, d, which):
        return way((4 - d) % 4) + which * (4 - 8 * zh)

    def index_of(which, half, d1, d2):
        return 1 + ((which * 2 + half) * 4 + d1) * 4 + d2

    sent = [move(block(fcol), 0, partner)]
    sent[0].start()
    near = (1, 3, 2)
    for which in range(2):
        base = fcol + which * (4 - 8 * zh)
        if which == 1:
            move(block(base), 0, partner).wait_recv()
        for stage in range(2):
            for half in range(2):
                for d in near:
                    key = index_of(which, half, d, 0) if stage == 0 else index_of(which, half, 0, d)
                    copy = move(block(base, half), key, routes[half][stage](d))
                    copy.start()
                    sent.append(copy)
        for d1 in near:
            for half in range(2):
                ref = block(source(routes[half][0], d1, which), half)
                move(ref, index_of(which, half, d1, 0), fcol).wait_recv()
                for d2 in near:
                    copy = move(ref, index_of(which, half, d1, d2), routes[half][1](d2))
                    copy.start()
                    sent.append(copy)
    for which in range(2):
        for half in range(2):
            for d1 in (0,) + near:
                for d2 in near:
                    move(block(fcol, half), index_of(which, half, d1, d2), fcol).wait_recv()
    for copy in sent:
        copy.wait_send()
    each(strips, "wait_send", 0)
    each(bands, "wait_send", 0)
    for n in range(2):
        each(corners[n], "wait_send", 0)


CHUNK = (9, 8, 7, 6, 5, 8)


def solution(mesh):
    n_row, n_col = mesh.shape["frow"], mesh.shape["fcol"]

    def body(right_side, noise_weight, stencils, neighbours):
        rows, cols, pix = right_side.shape
        slots = stencils.shape[0]
        ext = (rows + 2 * HALO, cols + 2 * SIDE)
        tiles = ext[0] * ext[1]
        listed = jnp.transpose(neighbours, (2, 0, 1))
        smooth, coarse = pl.pallas_call(
            functools.partial(kernel, (n_row, n_col, rows, cols, pix, slots)),
            out_shape=(
                jax.ShapeDtypeStruct((rows, cols, pix), jnp.float32),
                jax.ShapeDtypeStruct((rows // 2, cols // 2 * n_col, pix), jnp.bfloat16),
            ),
            in_specs=[pl.BlockSpec(memory_space=pl.ANY)] * 4,
            out_specs=(pl.BlockSpec(memory_space=pltpu.VMEM), pl.BlockSpec(memory_space=pltpu.VMEM)),
            scratch_shapes=[
                pltpu.VMEM(ext + (pix,), jnp.float32),
                pltpu.VMEM(ext + (pix,), jnp.float32),
                pltpu.VMEM((tiles, pix), jnp.float32),
                pltpu.VMEM((2, 3, tiles, pix), jnp.bfloat16),
                pltpu.VMEM((slots, tiles, 128), jnp.bfloat16),
                pltpu.VMEM((pix // 128, rows * ext[1], 128), jnp.float32),
                pltpu.VMEM((slots, rows, cols), jnp.int32),
                pltpu.VMEM((slots, pix, pix), jnp.bfloat16),
                pltpu.VMEM((2 * rows * cols + cols, pix), jnp.bfloat16),
                pltpu.VMEM((2, 2 * HALO * cols + cols, pix), jnp.bfloat16),
                pltpu.VMEM((2, 2 * rows * SIDE + 2 * SIDE, pix), jnp.bfloat16),
                pltpu.VMEM((2, 2 * rows * SIDE + 2 * SIDE, pix), jnp.bfloat16),
                pltpu.VMEM((4, 2 * HALO * SIDE + 2 * SIDE, pix), jnp.bfloat16),
                pltpu.SemaphoreType.DMA((4,)),
                pltpu.SemaphoreType.DMA((8,)),
                pltpu.SemaphoreType.DMA((8,)),
                pltpu.SemaphoreType.DMA((65,)),
                pltpu.SemaphoreType.DMA((65,)),
            ],
            compiler_params=pltpu.CompilerParams(
                collective_id=0, has_side_effects=True, vmem_limit_bytes=48 << 20
            ),
        )(*[pltpu.with_memory_space_constraint(v, pltpu.HBM) for v in (right_side, noise_weight, stencils, listed)])
        return smooth, coarse.astype(jnp.float32)

    placed = (P("frow", "fcol", None), P("frow", "fcol", None), P(), P("frow", "fcol", None))
    return jax.shard_map(
        body,
        mesh=mesh,
        in_specs=placed,
        out_specs=(P("frow", "fcol", None), P("frow", None, None)),
        check_vma=False,
    )
```

```python
import functools

import jax
import jax.numpy as jnp
from jax import lax
from jax.experimental import pallas as pl
from jax.experimental.pallas import tpu as pltpu
from jax.sharding import PartitionSpec as P

MESH = pl.DeviceIdType.MESH
LOWER, UPPER, DEG, SWEEPS = 1.5, 6.0, 3, 2
HALO = DEG * SWEEPS
SIDE = 8
MIDDLE = 3.75


def coefficients():
    center = 0.5 * (UPPER + LOWER)
    half_width = 0.5 * (UPPER - LOWER)
    spread = center / half_width
    steps = []
    for _ in range(SWEEPS):
        ratio = 1.0 / spread
        for step in range(DEG):
            if step < DEG - 1:
                after = 1.0 / (2.0 * spread - ratio)
                steps.append((after * ratio, 2.0 * after / half_width))
                ratio = after
            else:
                steps.append((0.0, 1.0 / center))
    return center, steps


def kernel(
    sizes, rs, nw, st, nb, sol_ref, out_ref, res, wgt, drc, dir_bf, msk, fin, own_nb, stv,
    band_out, band_in, strip_out, strip_in, corner_in, loc_sem, h_send, h_recv, g_send, g_recv
):
    n_row, n_col, rows, cols, pix, slots = sizes
    ext_rows, ext_cols = rows + 2 * HALO, cols + 2 * SIDE
    frow, fcol = lax.axis_index("frow"), lax.axis_index("fcol")
    f32, bf16 = jnp.float32, jnp.bfloat16
    has = {"up": frow > 0, "down": frow < n_row - 1, "left": fcol > 0, "right": fcol < n_col - 1}
    beside = {"up": (frow - 1, fcol), "down": (frow + 1, fcol), "left": (frow, fcol - 1), "right": (frow, fcol + 1)}
    sides = ("up", "down", "left", "right")
    y, zh = lax.rem(fcol, 4), lax.rem(fcol // 4, 2)

    def along_x(d):
        return lax.rem(fcol + 8 * d, n_col)

    def along_y(d):
        return fcol - y + lax.rem(y + d, 4)

    partner = fcol + 4 - 8 * zh

    barrier = pltpu.get_barrier_semaphore()
    for side in sides:

        @pl.when(has[side])
        def _(side=side):
            pl.semaphore_signal(barrier, inc=1, device_id=beside[side], device_id_type=MESH)

    for peer in [along_x(d) for d in (1, 2, 3)] + [along_y(d) for d in (1, 2, 3)] + [partner]:
        pl.semaphore_signal(barrier, inc=1, device_id=(frow, peer), device_id_type=MESH)

    local = [
        pltpu.make_async_copy(nb, own_nb, loc_sem.at[0]),
        pltpu.make_async_copy(rs, res.at[pl.ds(HALO, rows), pl.ds(SIDE, cols)], loc_sem.at[1]),
        pltpu.make_async_copy(nw, wgt.at[pl.ds(HALO, rows), pl.ds(SIDE, cols)], loc_sem.at[2]),
        pltpu.make_async_copy(st, stv, loc_sem.at[3]),
    ]
    for copy in local:
        copy.start()

    for n, side in enumerate(("up", "down")):

        @pl.when(jnp.logical_not(has[side]))
        def _(n=n):
            band_in[n] = jnp.zeros(band_in.shape[1:], bf16)
            corner_in[2 * n] = jnp.zeros(corner_in.shape[1:], bf16)
            corner_in[2 * n + 1] = jnp.zeros(corner_in.shape[1:], bf16)

    for n, side in enumerate(("left", "right")):

        @pl.when(jnp.logical_not(has[side]))
        def _(n=n):
            strip_in[n] = jnp.zeros(strip_in.shape[1:], bf16)

    for copy in local[:3]:
        copy.wait()
    flat = jnp.where(own_nb[...] >= 0, 1.0, 0.0).astype(f32).reshape(slots * rows, cols)
    flat = jnp.concatenate([flat, jnp.zeros((128 - slots * rows, cols), f32)], axis=0)
    turned = jnp.transpose(flat)
    listed = jnp.concatenate([turned, jnp.zeros((cols, pix - 128), f32)], axis=1)
    half = rows // 2 - 1
    unit, small = 2 * cols, 2 * SIDE

    def spot(row, size, middle):
        return row * size + (middle if row >= half else 0)

    for n, c0 in ((0, 0), (1, cols - SIDE)):
        strip_out[n, pl.ds(half * small, small), :] = jnp.concatenate(
            [listed[c0 : c0 + SIDE], jnp.zeros((SIDE, pix), f32)], axis=0
        ).astype(bf16)
    for row in range(rows):
        for n, c0 in ((0, 0), (1, cols - SIDE)):
            strip_out[n, pl.ds(spot(row, small, small), small), :] = jnp.concatenate(
                [
                    res[HALO + row, pl.ds(SIDE + c0, SIDE), :],
                    wgt[HALO + row, pl.ds(SIDE + c0, SIDE), :] - MIDDLE,
                ],
                axis=0,
            ).astype(bf16)

    band_size = HALO * unit + cols
    corner_size = HALO * small + small

    def remote(src, dst, index, peer):
        return pltpu.make_async_remote_copy(
            src_ref=src, dst_ref=dst, send_sem=h_send.at[index], recv_sem=h_recv.at[index],
            device_id=peer, device_id_type=MESH,
        )

    far_band, far_strip = pl.ds((rows - HALO) * unit, band_size), pl.ds((rows - HALO) * small, corner_size)
    near_band, near_strip = pl.ds(0, band_size), pl.ds(0, corner_size)
    strips = [
        ("right", "left", lambda: remote(strip_out.at[1], strip_in.at[0], 0, beside["right"])),
        ("left", "right", lambda: remote(strip_out.at[0], strip_in.at[1], 1, beside["left"])),
    ]
    bands = [
        ("down", "up", lambda: remote(band_out.at[far_band], band_in.at[0], 2, beside["down"])),
        ("up", "down", lambda: remote(band_out.at[near_band], band_in.at[1], 3, beside["up"])),
    ]
    corners = [
        [
            ("down", "up", lambda n=n: remote(strip_in.at[n, far_strip], corner_in.at[n], 4 + n, beside["down"])),
            ("up", "down", lambda n=n: remote(strip_in.at[n, near_strip], corner_in.at[2 + n], 6 + n, beside["up"])),
        ]
        for n in range(2)
    ]

    def each(copies, act, by):
        for entry in copies:

            @pl.when(has[entry[by]])
            def _(entry=entry):
                getattr(entry[2](), act)()

    amount = 7
    for side in sides:
        amount = amount + jnp.where(has[side], 1, 0)
    pl.semaphore_wait(barrier, amount)
    each(strips, "start", 0)
    band_out[pl.ds(half * unit, cols), :] = listed.astype(bf16)
    for row in range(rows):
        r = res[HALO + row, pl.ds(SIDE, cols), :]
        w = wgt[HALO + row, pl.ds(SIDE, cols), :] - MIDDLE
        band_out[pl.ds(spot(row, unit, cols), unit), :] = jnp.concatenate([r, w], axis=0).astype(bf16)
    each(bands, "start", 0)

    def mask_rows(first, last, base, left, middle, right):
        whole = jnp.concatenate([left.astype(f32)[:SIDE, :128], middle, right.astype(f32)[:SIDE, :128]], axis=0)
        for k in range(slots):
            for row in range(first, last):
                m = k * rows + row
                wide = jnp.broadcast_to(whole[:, m : m + 1], (ext_cols, 128)).astype(bf16)
                msk[k, pl.ds((base + row - first) * ext_cols, ext_cols), :] = wide

    for n in range(2):
        each(strips[n : n + 1], "wait_recv", 1)
        each(corners[n], "start", 0)
    for m, c0 in ((0, 0), (1, SIDE + cols)):
        for row in range(rows):
            part = strip_in[m, pl.ds(spot(row, small, small), small), :].astype(f32)
            res[HALO + row, pl.ds(c0, SIDE), :] = part[:SIDE]
            wgt[HALO + row, pl.ds(c0, SIDE), :] = part[SIDE:] + MIDDLE
    mask_rows(
        0, rows, HALO, strip_in[0, pl.ds(half * small, small), :], turned, strip_in[1, pl.ds(half * small, small), :]
    )
    each(bands, "wait_recv", 1)
    both = ((0, 0, rows - HALO), (1, HALO + rows, 0))
    for n, base, skip in both:
        for i in range(HALO):
            part = band_in[n, pl.ds(spot(i + skip, unit, cols) - skip * unit, unit), :].astype(f32)
            res[base + i, pl.ds(SIDE, cols), :] = part[:cols]
            wgt[base + i, pl.ds(SIDE, cols), :] = part[cols:] + MIDDLE
    for n in range(2):
        each(corners[n], "wait_recv", 1)
    for n, base, skip in both:
        for i in range(HALO):
            for m, c0 in ((0, 0), (1, SIDE + cols)):
                part = corner_in[2 * n + m, pl.ds(spot(i + skip, small, small) - skip * small, small), :].astype(f32)
                res[base + i, pl.ds(c0, SIDE), :] = part[:SIDE]
                wgt[base + i, pl.ds(c0, SIDE), :] = part[SIDE:] + MIDDLE
        kept = half - skip
        mask_rows(
            skip, skip + HALO, base,
            corner_in[2 * n, pl.ds(kept * small, small), :],
            band_in[n, pl.ds(kept * unit, cols), :].astype(f32)[:, :128],
            corner_in[2 * n + 1, pl.ds(kept * small, small), :],
        )
    local[3].wait()

    center, steps = coefficients()

    def put(buf, t0, count, value):
        for j, shift in enumerate((1, 0, count - 1)):
            moved = value if shift == 0 else pltpu.roll(value, shift, axis=0)
            dir_bf[buf, j, pl.ds(t0, count), :] = moved.astype(jnp.bfloat16)

    res_flat = res.reshape(ext_rows * ext_cols, pix)
    wgt_flat = wgt.reshape(ext_rows * ext_cols, pix)

    def begin(i, c):
        t0 = pl.multiple_of(i * (2 * ext_cols), 2 * ext_cols)
        d = res_flat[pl.ds(t0, 2 * ext_cols), :] * (1.0 / center)
        drc[pl.ds(t0, 2 * ext_cols), :] = d
        put(0, t0, 2 * ext_cols, d)
        return c

    lax.fori_loop(0, ext_rows // 2, begin, 0)

    drc_cube = drc.reshape(ext_rows, ext_cols, pix)

    for op in range(HALO):
        now, later = op % 2, (op + 1) % 2
        low = op + 1
        count = ext_rows - 2 * low
        chunk = CHUNK[op]
        size = chunk * ext_cols
        own = drc_cube[pl.ds(HALO, rows), pl.ds(SIDE, cols), :]
        sol_ref[...] = own if op == 0 else sol_ref[...] + own

        def apply(i, c, now=now, later=later, low=low, size=size, op=op):
            t0 = pl.multiple_of(low * ext_cols + i * size, ext_cols)
            parts = []
            for k in range(slots):
                src = t0 + (k // 3 - 1) * ext_cols
                part = dir_bf[now, k % 3, pl.ds(pl.multiple_of(src, ext_cols), size), :]
                keep = msk[k, pl.ds(t0, size), :]
                parts.append(part * jnp.concatenate([keep, keep], axis=1))
            coupled = jnp.dot(
                jnp.concatenate(parts, axis=1), stv[...].reshape(slots * pix, pix), preferred_element_type=jnp.float32
            )
            d = drc[pl.ds(t0, size), :]
            r = res_flat[pl.ds(t0, size), :] - (wgt_flat[pl.ds(t0, size), :] * d + coupled)
            if op == HALO - 1:
                for h in range(pix // 128):
                    fin[h] = r[:, h * 128 : (h + 1) * 128]
            else:
                res_flat[pl.ds(t0, size), :] = r
                old, new = steps[op]
                d = new * r if old == 0.0 else old * d + new * r
                drc[pl.ds(t0, size), :] = d
                put(later, t0, size, d)
            return c

        trips = count // chunk
        if trips == 1:
            apply(0, 0)
        else:
            lax.fori_loop(0, trips, apply, 0)

    pixel = lax.broadcasted_iota(jnp.int32, (pix, 128), 0)
    lane = lax.broadcasted_iota(jnp.int32, (pix, 128), 1)
    fold = jnp.where(pixel // 4 == lane % 64, 1.0, 0.0).astype(jnp.bfloat16)
    pieces = []
    for a in range(2):
        for b in range(2):
            for R in range(rows // 2):
                begin_at = (2 * R + a) * ext_cols + SIDE + b
                pieces.append(
                    jnp.concatenate(
                        [fin[h, pl.ds(begin_at, cols // 2, stride=2), :] for h in range(pix // 128)], axis=1
                    )
                )
    stack = jnp.concatenate(pieces, axis=0)
    high = stack.astype(jnp.bfloat16)
    low_part = (stack - high.astype(jnp.float32)).astype(jnp.bfloat16)
    summed = jnp.dot(high, fold, preferred_element_type=jnp.float32) + jnp.dot(
        low_part, fold, preferred_element_type=jnp.float32
    )
    quarter = (rows // 2) * (cols // 2)
    quads = [summed[q * quarter : (q + 1) * quarter] for q in range(4)]
    left = lax.broadcasted_iota(jnp.int32, (quarter, 128), 1) < 64
    coarse = jnp.concatenate([jnp.where(left, quads[0], quads[1]), jnp.where(left, quads[2], quads[3])], axis=1).astype(jnp.bfloat16)
    quarter_cols = cols // 2
    group = rows // 4

    def block(j, half=None):
        span = pl.ds(pl.multiple_of(j * quarter_cols, quarter_cols), quarter_cols)
        if half is None:
            return out_ref.at[:, span, :]
        return out_ref.at[pl.ds(half * group, group), span, :]

    out_ref[:, pl.ds(pl.multiple_of(fcol * quarter_cols, quarter_cols), quarter_cols), :] = coarse.reshape(
        rows // 2, quarter_cols, pix
    )

    def move(ref, index, peer):
        return pltpu.make_async_remote_copy(
            src_ref=ref, dst_ref=ref, send_sem=g_send.at[index], recv_sem=g_recv.at[index],
            device_id=(frow, peer), device_id_type=MESH,
        )

    routes = ((along_x, along_y), (along_y, along_x))

    def source(way, d, which):
        return way((4 - d) % 4) + which * (4 - 8 * zh)

    def index_of(which, half, d1, d2):
        return 1 + ((which * 2 + half) * 4 + d1) * 4 + d2

    sent = [move(block(fcol), 0, partner)]
    sent[0].start()
    near = (1, 3, 2)
    for which in range(2):
        base = fcol + which * (4 - 8 * zh)
        if which == 1:
            move(block(base), 0, partner).wait_recv()
        for stage in range(2):
            for half in range(2):
                for d in near:
                    key = index_of(which, half, d, 0) if stage == 0 else index_of(which, half, 0, d)
                    copy = move(block(base, half), key, routes[half][stage](d))
                    copy.start()
                    sent.append(copy)
        for d1 in near:
            for half in range(2):
                ref = block(source(routes[half][0], d1, which), half)
                move(ref, index_of(which, half, d1, 0), fcol).wait_recv()
                for d2 in near:
                    copy = move(ref, index_of(which, half, d1, d2), routes[half][1](d2))
                    copy.start()
                    sent.append(copy)
    for which in range(2):
        for half in range(2):
            for d1 in (0,) + near:
                for d2 in near:
                    move(block(fcol, half), index_of(which, half, d1, d2), fcol).wait_recv()
    for copy in sent:
        copy.wait_send()
    each(strips, "wait_send", 0)
    each(bands, "wait_send", 0)
    for n in range(2):
        each(corners[n], "wait_send", 0)


CHUNK = (9, 8, 7, 6, 5, 8)


def widen_kernel(smooth_in, coarse_in, smooth_out, coarse_out, wide, sems):
    first = pltpu.make_async_copy(smooth_in, smooth_out, sems.at[0])
    first.start()
    copies = []
    for i in range(coarse_in.shape[0]):
        wide[i] = coarse_in[i].astype(jnp.float32)
        copy = pltpu.make_async_copy(wide.at[i], coarse_out.at[i], sems.at[1 + i])
        copy.start()
        copies.append(copy)
    first.wait()
    for copy in copies:
        copy.wait()


def widen(smooth, coarse):
    return pl.pallas_call(
        widen_kernel,
        out_shape=(
            jax.ShapeDtypeStruct(smooth.shape, jnp.float32),
            jax.ShapeDtypeStruct(coarse.shape, jnp.float32),
        ),
        in_specs=[pl.BlockSpec(memory_space=pltpu.VMEM)] * 2,
        out_specs=[pl.BlockSpec(memory_space=pltpu.HBM)] * 2,
        scratch_shapes=[pltpu.VMEM(coarse.shape, jnp.float32), pltpu.SemaphoreType.DMA((1 + coarse.shape[0],))],
        compiler_params=pltpu.CompilerParams(vmem_limit_bytes=32 << 20),
    )(smooth, coarse)


def solution(mesh):
    n_row, n_col = mesh.shape["frow"], mesh.shape["fcol"]

    def body(right_side, noise_weight, stencils, neighbours):
        rows, cols, pix = right_side.shape
        slots = stencils.shape[0]
        ext = (rows + 2 * HALO, cols + 2 * SIDE)
        tiles = ext[0] * ext[1]
        listed = jnp.transpose(neighbours, (2, 0, 1))
        smooth, coarse = pl.pallas_call(
            functools.partial(kernel, (n_row, n_col, rows, cols, pix, slots)),
            out_shape=(
                jax.ShapeDtypeStruct((rows, cols, pix), jnp.float32),
                jax.ShapeDtypeStruct((rows // 2, cols // 2 * n_col, pix), jnp.bfloat16),
            ),
            in_specs=[pl.BlockSpec(memory_space=pl.ANY)] * 4,
            out_specs=(pl.BlockSpec(memory_space=pltpu.VMEM), pl.BlockSpec(memory_space=pltpu.VMEM)),
            scratch_shapes=[
                pltpu.VMEM(ext + (pix,), jnp.float32),
                pltpu.VMEM(ext + (pix,), jnp.float32),
                pltpu.VMEM((tiles, pix), jnp.float32),
                pltpu.VMEM((2, 3, tiles, pix), jnp.bfloat16),
                pltpu.VMEM((slots, tiles, 128), jnp.bfloat16),
                pltpu.VMEM((pix // 128, rows * ext[1], 128), jnp.float32),
                pltpu.VMEM((slots, rows, cols), jnp.int32),
                pltpu.VMEM((slots, pix, pix), jnp.bfloat16),
                pltpu.VMEM((2 * rows * cols + cols, pix), jnp.bfloat16),
                pltpu.VMEM((2, 2 * HALO * cols + cols, pix), jnp.bfloat16),
                pltpu.VMEM((2, 2 * rows * SIDE + 2 * SIDE, pix), jnp.bfloat16),
                pltpu.VMEM((2, 2 * rows * SIDE + 2 * SIDE, pix), jnp.bfloat16),
                pltpu.VMEM((4, 2 * HALO * SIDE + 2 * SIDE, pix), jnp.bfloat16),
                pltpu.SemaphoreType.DMA((4,)),
                pltpu.SemaphoreType.DMA((8,)),
                pltpu.SemaphoreType.DMA((8,)),
                pltpu.SemaphoreType.DMA((65,)),
                pltpu.SemaphoreType.DMA((65,)),
            ],
            compiler_params=pltpu.CompilerParams(
                collective_id=0, has_side_effects=True, vmem_limit_bytes=48 << 20,
            ),
        )(*[pltpu.with_memory_space_constraint(v, pltpu.HBM) for v in (right_side, noise_weight, stencils, listed)])
        return widen(smooth, coarse)

    placed = (P("frow", "fcol", None), P("frow", "fcol", None), P(), P("frow", "fcol", None))
    return jax.shard_map(
        body,
        mesh=mesh,
        in_specs=placed,
        out_specs=(P("frow", "fcol", None), P("frow", None, None)),
        check_vma=False,
    )
```

```python
import functools

import jax
import jax.numpy as jnp
from jax import lax
from jax.experimental import pallas as pl
from jax.experimental.pallas import tpu as pltpu
from jax.sharding import PartitionSpec as P

MESH = pl.DeviceIdType.MESH
LOWER, UPPER, DEG, SWEEPS = 1.5, 6.0, 3, 2
HALO = DEG * SWEEPS
SIDE = 8
MIDDLE = 3.75


def coefficients():
    center = 0.5 * (UPPER + LOWER)
    half_width = 0.5 * (UPPER - LOWER)
    spread = center / half_width
    steps = []
    for _ in range(SWEEPS):
        ratio = 1.0 / spread
        for step in range(DEG):
            if step < DEG - 1:
                after = 1.0 / (2.0 * spread - ratio)
                steps.append((after * ratio, 2.0 * after / half_width))
                ratio = after
            else:
                steps.append((0.0, 1.0 / center))
    return center, steps


def kernel(
    sizes, rs, nw, st, nb, sol_ref, out_ref, res, wgt, drc, dir_bf, msk, fin, own_nb, stv,
    band_out, band_in, strip_out, strip_in, corner_in, kept, loc_sem, h_send, h_recv, g_send, g_recv, k_send, k_recv, partner_in, asked
):
    n_row, n_col, rows, cols, pix, slots = sizes
    ext_rows, ext_cols = rows + 2 * HALO, cols + 2 * SIDE
    frow, fcol = lax.axis_index("frow"), lax.axis_index("fcol")
    f32, bf16 = jnp.float32, jnp.bfloat16
    has = {"up": frow > 0, "down": frow < n_row - 1, "left": fcol > 0, "right": fcol < n_col - 1}
    beside = {"up": (frow - 1, fcol), "down": (frow + 1, fcol), "left": (frow, fcol - 1), "right": (frow, fcol + 1)}
    sides = ("up", "down", "left", "right")
    y, zh = lax.rem(fcol, 4), lax.rem(fcol // 4, 2)

    def along_x(d):
        return lax.rem(fcol + 8 * d, n_col)

    def along_y(d):
        return fcol - y + lax.rem(y + d, 4)

    partner = fcol + 4 - 8 * zh

    level, core = frow // 2, lax.rem(frow, 2)
    early, late = zh == 0, zh == 1
    first, last = y == 0, y == 3
    far = jnp.logical_or(jnp.logical_and(first, has["left"]), jnp.logical_and(last, has["right"]))
    gives, gets = jnp.logical_and(early, far), jnp.logical_and(late, far)
    ends = jnp.logical_or(level == 0, level == 3)
    keeps = jnp.logical_and(
        jnp.logical_and(early, ends), jnp.logical_or(first, jnp.logical_and(last, fcol < n_col - 5))
    )
    keeper_row = jnp.where(level < 2, 6, 0) + core
    keeper_of_giver = (keeper_row, jnp.where(last, fcol - 3, fcol - 5))
    keeper_of_getter = (keeper_row, fcol - 4)
    kept_rows = [jnp.where(level == 3, 0, 4) + 2 * i + core for i in range(2)]
    giver_col, getter_col = jnp.where(first, fcol + 3, fcol + 5), fcol + 4
    side_in = jnp.where(first, 0, 1)

    def hail(sem, peer):
        pl.semaphore_signal(sem, inc=1, device_id=peer, device_id_type=MESH)

    barrier = pltpu.get_barrier_semaphore()
    known = {
        "up": has["up"],
        "down": has["down"],
        "left": jnp.logical_and(has["left"], jnp.logical_not(jnp.logical_and(late, first))),
        "right": jnp.logical_and(has["right"], jnp.logical_not(jnp.logical_and(late, last))),
    }
    for side in sides:

        @pl.when(known[side])
        def _(side=side):
            hail(barrier, beside[side])

    for peer in [along_x(d) for d in (1, 2, 3)] + [along_y(d) for d in (1, 2, 3)]:
        hail(barrier, (frow, peer))

    @pl.when(early)
    def _():
        hail(barrier, (frow, partner))

    @pl.when(keeps)
    def _():
        for row in kept_rows:
            hail(barrier, (row, getter_col))
            hail(barrier, (row, giver_col))

    local = [
        pltpu.make_async_copy(nb, own_nb, loc_sem.at[0]),
        pltpu.make_async_copy(rs, res.at[pl.ds(HALO, rows), pl.ds(SIDE, cols)], loc_sem.at[1]),
        pltpu.make_async_copy(nw, wgt.at[pl.ds(HALO, rows), pl.ds(SIDE, cols)], loc_sem.at[2]),
        pltpu.make_async_copy(st, stv, loc_sem.at[3]),
    ]
    for copy in local:
        copy.start()

    for n, side in enumerate(("up", "down")):

        @pl.when(jnp.logical_not(has[side]))
        def _(n=n):
            band_in[n] = jnp.zeros(band_in.shape[1:], bf16)
            corner_in[2 * n] = jnp.zeros(corner_in.shape[1:], bf16)
            corner_in[2 * n + 1] = jnp.zeros(corner_in.shape[1:], bf16)

    for n, side in enumerate(("left", "right")):

        @pl.when(jnp.logical_not(has[side]))
        def _(n=n):
            strip_in[n] = jnp.zeros(strip_in.shape[1:], bf16)

    for copy in local[:3]:
        copy.wait()
    flat = jnp.where(own_nb[...] >= 0, 1.0, 0.0).astype(f32).reshape(slots * rows, cols)
    flat = jnp.concatenate([flat, jnp.zeros((128 - slots * rows, cols), f32)], axis=0)
    turned = jnp.transpose(flat)
    listed = jnp.concatenate([turned, jnp.zeros((cols, pix - 128), f32)], axis=1)
    half = rows // 2 - 1
    unit, small = 2 * cols, 2 * SIDE

    def spot(row, size, middle):
        return row * size + (middle if row >= half else 0)

    for n, c0 in ((0, 0), (1, cols - SIDE)):
        strip_out[n, pl.ds(half * small, small), :] = jnp.concatenate(
            [listed[c0 : c0 + SIDE], jnp.zeros((SIDE, pix), f32)], axis=0
        ).astype(bf16)
    for row in range(rows):
        for n, c0 in ((0, 0), (1, cols - SIDE)):
            strip_out[n, pl.ds(spot(row, small, small), small), :] = jnp.concatenate(
                [
                    res[HALO + row, pl.ds(SIDE + c0, SIDE), :],
                    wgt[HALO + row, pl.ds(SIDE + c0, SIDE), :] - MIDDLE,
                ],
                axis=0,
            ).astype(bf16)

    band_size = HALO * unit + cols
    corner_size = HALO * small + small

    def remote(src, dst, index, peer):
        return pltpu.make_async_remote_copy(
            src_ref=src, dst_ref=dst, send_sem=h_send.at[index], recv_sem=h_recv.at[index],
            device_id=peer, device_id_type=MESH,
        )

    far_band, far_strip = pl.ds((rows - HALO) * unit, band_size), pl.ds((rows - HALO) * small, corner_size)
    near_band, near_strip = pl.ds(0, band_size), pl.ds(0, corner_size)
    strips = [
        ("right", "left", lambda: remote(strip_out.at[1], strip_in.at[0], 0, beside["right"])),
        ("left", "right", lambda: remote(strip_out.at[0], strip_in.at[1], 1, beside["left"])),
    ]
    bands = [
        ("down", "up", lambda: remote(band_out.at[far_band], band_in.at[0], 2, beside["down"])),
        ("up", "down", lambda: remote(band_out.at[near_band], band_in.at[1], 3, beside["up"])),
    ]
    corners = [
        [
            ("down", "up", lambda n=n: remote(strip_in.at[n, far_strip], corner_in.at[n], 4 + n, beside["down"])),
            ("up", "down", lambda n=n: remote(strip_in.at[n, near_strip], corner_in.at[2 + n], 6 + n, beside["up"])),
        ]
        for n in range(2)
    ]

    def each(copies, act, by):
        for entry in copies:

            @pl.when(has[entry[by]])
            def _(entry=entry):
                getattr(entry[2](), act)()

    direct = {
        "left": jnp.logical_and(has["left"], jnp.logical_not(jnp.logical_and(early, first))),
        "right": jnp.logical_and(has["right"], jnp.logical_not(jnp.logical_and(early, last))),
    }
    amount = 6
    for side in ("up", "down"):
        amount = amount + jnp.where(has[side], 1, 0)
    for side in ("left", "right"):
        amount = amount + jnp.where(jnp.where(late, has[side], direct[side]), 1, 0)
    amount = amount + jnp.where(late, 1, 0) + jnp.where(far, 1, 0)
    pl.semaphore_wait(barrier, amount)

    @pl.when(late)
    def _():
        hail(partner_in, (frow, partner))

    @pl.when(gets)
    def _():
        hail(asked.at[lax.rem(level, 2)], keeper_of_getter)

    def ahead():
        slot = lax.rem(level, 2)
        return pltpu.make_async_remote_copy(
            src_ref=strip_out.at[side_in], dst_ref=kept.at[slot], send_sem=k_send.at[0], recv_sem=k_recv.at[slot],
            device_id=keeper_of_giver, device_id_type=MESH,
        )

    def onward(i):
        return pltpu.make_async_remote_copy(
            src_ref=kept.at[i], dst_ref=strip_in.at[side_in], send_sem=k_send.at[1 + i], recv_sem=h_recv.at[side_in],
            device_id=(kept_rows[i], getter_col), device_id_type=MESH,
        )

    @pl.when(gives)
    def _():
        ahead().start()

    for entry in strips:

        @pl.when(direct[entry[0]])
        def _(entry=entry):
            entry[2]().start()

    band_out[pl.ds(half * unit, cols), :] = listed.astype(bf16)
    for row in range(rows):
        r = res[HALO + row, pl.ds(SIDE, cols), :]
        w = wgt[HALO + row, pl.ds(SIDE, cols), :] - MIDDLE
        band_out[pl.ds(spot(row, unit, cols), unit), :] = jnp.concatenate([r, w], axis=0).astype(bf16)
    each(bands, "start", 0)

    @pl.when(keeps)
    def _():
        for i in range(2):
            pltpu.make_async_remote_copy(
                src_ref=kept.at[i], dst_ref=kept.at[i], send_sem=k_send.at[0], recv_sem=k_recv.at[i],
                device_id=(kept_rows[i], giver_col), device_id_type=MESH,
            ).wait_recv()
        for i in range(2):
            pl.semaphore_wait(asked.at[i], 1)
            onward(i).start()

    def mask_rows(first, last, base, left, middle, right):
        whole = jnp.concatenate([left.astype(f32)[:SIDE, :128], middle, right.astype(f32)[:SIDE, :128]], axis=0)
        for k in range(slots):
            for row in range(first, last):
                m = k * rows + row
                wide = jnp.broadcast_to(whole[:, m : m + 1], (ext_cols, 128)).astype(bf16)
                msk[k, pl.ds((base + row - first) * ext_cols, ext_cols), :] = wide

    for n in range(2):
        each(strips[n : n + 1], "wait_recv", 1)
        each(corners[n], "start", 0)
    for m, c0 in ((0, 0), (1, SIDE + cols)):
        for row in range(rows):
            part = strip_in[m, pl.ds(spot(row, small, small), small), :].astype(f32)
            res[HALO + row, pl.ds(c0, SIDE), :] = part[:SIDE]
            wgt[HALO + row, pl.ds(c0, SIDE), :] = part[SIDE:] + MIDDLE
    mask_rows(
        0, rows, HALO, strip_in[0, pl.ds(half * small, small), :], turned, strip_in[1, pl.ds(half * small, small), :]
    )
    each(bands, "wait_recv", 1)
    both = ((0, 0, rows - HALO), (1, HALO + rows, 0))
    for n, base, skip in both:
        for i in range(HALO):
            part = band_in[n, pl.ds(spot(i + skip, unit, cols) - skip * unit, unit), :].astype(f32)
            res[base + i, pl.ds(SIDE, cols), :] = part[:cols]
            wgt[base + i, pl.ds(SIDE, cols), :] = part[cols:] + MIDDLE
    for n in range(2):
        each(corners[n], "wait_recv", 1)
    for n, base, skip in both:
        for i in range(HALO):
            for m, c0 in ((0, 0), (1, SIDE + cols)):
                part = corner_in[2 * n + m, pl.ds(spot(i + skip, small, small) - skip * small, small), :].astype(f32)
                res[base + i, pl.ds(c0, SIDE), :] = part[:SIDE]
                wgt[base + i, pl.ds(c0, SIDE), :] = part[SIDE:] + MIDDLE
        offset = half - skip
        mask_rows(
            skip, skip + HALO, base,
            corner_in[2 * n, pl.ds(offset * small, small), :],
            band_in[n, pl.ds(offset * unit, cols), :].astype(f32)[:, :128],
            corner_in[2 * n + 1, pl.ds(offset * small, small), :],
        )
    local[3].wait()

    center, steps = coefficients()

    def put(buf, t0, count, value):
        for j, shift in enumerate((1, 0, count - 1)):
            moved = value if shift == 0 else pltpu.roll(value, shift, axis=0)
            dir_bf[buf, j, pl.ds(t0, count), :] = moved.astype(jnp.bfloat16)

    res_flat = res.reshape(ext_rows * ext_cols, pix)
    wgt_flat = wgt.reshape(ext_rows * ext_cols, pix)

    def begin(i, c):
        t0 = pl.multiple_of(i * (2 * ext_cols), 2 * ext_cols)
        d = res_flat[pl.ds(t0, 2 * ext_cols), :] * (1.0 / center)
        drc[pl.ds(t0, 2 * ext_cols), :] = d
        put(0, t0, 2 * ext_cols, d)
        return c

    lax.fori_loop(0, ext_rows // 2, begin, 0)

    drc_cube = drc.reshape(ext_rows, ext_cols, pix)

    for op in range(HALO):
        now, later = op % 2, (op + 1) % 2
        low = op + 1
        count = ext_rows - 2 * low
        chunk = CHUNK[op]
        size = chunk * ext_cols
        own = drc_cube[pl.ds(HALO, rows), pl.ds(SIDE, cols), :]
        sol_ref[...] = own if op == 0 else sol_ref[...] + own

        def apply(i, c, now=now, later=later, low=low, size=size, op=op):
            t0 = pl.multiple_of(low * ext_cols + i * size, ext_cols)
            parts = []
            for k in range(slots):
                src = t0 + (k // 3 - 1) * ext_cols
                part = dir_bf[now, k % 3, pl.ds(pl.multiple_of(src, ext_cols), size), :]
                keep = msk[k, pl.ds(t0, size), :]
                parts.append(part * jnp.concatenate([keep, keep], axis=1))
            coupled = jnp.dot(
                jnp.concatenate(parts, axis=1), stv[...].reshape(slots * pix, pix), preferred_element_type=jnp.float32
            )
            d = drc[pl.ds(t0, size), :]
            r = res_flat[pl.ds(t0, size), :] - (wgt_flat[pl.ds(t0, size), :] * d + coupled)
            if op == HALO - 1:
                for h in range(pix // 128):
                    fin[h] = r[:, h * 128 : (h + 1) * 128]
            else:
                res_flat[pl.ds(t0, size), :] = r
                old, new = steps[op]
                d = new * r if old == 0.0 else old * d + new * r
                drc[pl.ds(t0, size), :] = d
                put(later, t0, size, d)
            return c

        trips = count // chunk
        if trips == 1:
            apply(0, 0)
        else:
            lax.fori_loop(0, trips, apply, 0)

    pixel = lax.broadcasted_iota(jnp.int32, (pix, 128), 0)
    lane = lax.broadcasted_iota(jnp.int32, (pix, 128), 1)
    fold = jnp.where(pixel // 4 == lane % 64, 1.0, 0.0).astype(jnp.bfloat16)
    pieces = []
    for a in range(2):
        for b in range(2):
            for R in range(rows // 2):
                begin_at = (2 * R + a) * ext_cols + SIDE + b
                pieces.append(
                    jnp.concatenate(
                        [fin[h, pl.ds(begin_at, cols // 2, stride=2), :] for h in range(pix // 128)], axis=1
                    )
                )
    stack = jnp.concatenate(pieces, axis=0)
    high = stack.astype(jnp.bfloat16)
    low_part = (stack - high.astype(jnp.float32)).astype(jnp.bfloat16)
    summed = jnp.dot(high, fold, preferred_element_type=jnp.float32) + jnp.dot(
        low_part, fold, preferred_element_type=jnp.float32
    )
    quarter = (rows // 2) * (cols // 2)
    quads = [summed[q * quarter : (q + 1) * quarter] for q in range(4)]
    left = lax.broadcasted_iota(jnp.int32, (quarter, 128), 1) < 64
    coarse = jnp.concatenate([jnp.where(left, quads[0], quads[1]), jnp.where(left, quads[2], quads[3])], axis=1).astype(jnp.bfloat16)
    quarter_cols = cols // 2
    group = rows // 4

    def block(j, half=None):
        span = pl.ds(pl.multiple_of(j * quarter_cols, quarter_cols), quarter_cols)
        if half is None:
            return out_ref.at[:, span, :]
        return out_ref.at[pl.ds(half * group, group), span, :]

    out_ref[:, pl.ds(pl.multiple_of(fcol * quarter_cols, quarter_cols), quarter_cols), :] = coarse.reshape(
        rows // 2, quarter_cols, pix
    )

    def move(ref, index, peer):
        return pltpu.make_async_remote_copy(
            src_ref=ref, dst_ref=ref, send_sem=g_send.at[index], recv_sem=g_recv.at[index],
            device_id=(frow, peer), device_id_type=MESH,
        )

    routes = ((along_x, along_y), (along_y, along_x))

    def source(way, d, which):
        return way((4 - d) % 4) + which * (4 - 8 * zh)

    def index_of(which, half, d1, d2):
        return 1 + ((which * 2 + half) * 4 + d1) * 4 + d2

    sent = [move(block(fcol), 0, partner)]

    @pl.when(early)
    def _():
        pl.semaphore_wait(partner_in, 1)

    sent[0].start()
    near = (1, 3, 2)
    for which in range(2):
        base = fcol + which * (4 - 8 * zh)
        if which == 1:
            move(block(base), 0, partner).wait_recv()
        for stage in range(2):
            for half in range(2):
                for d in near:
                    key = index_of(which, half, d, 0) if stage == 0 else index_of(which, half, 0, d)
                    copy = move(block(base, half), key, routes[half][stage](d))
                    copy.start()
                    sent.append(copy)
        for d1 in near:
            for half in range(2):
                ref = block(source(routes[half][0], d1, which), half)
                move(ref, index_of(which, half, d1, 0), fcol).wait_recv()
                for d2 in near:
                    copy = move(ref, index_of(which, half, d1, d2), routes[half][1](d2))
                    copy.start()
                    sent.append(copy)
    for which in range(2):
        for half in range(2):
            for d1 in (0,) + near:
                for d2 in near:
                    move(block(fcol, half), index_of(which, half, d1, d2), fcol).wait_recv()
    for copy in sent:
        copy.wait_send()
    for entry in strips:

        @pl.when(direct[entry[0]])
        def _(entry=entry):
            entry[2]().wait_send()

    @pl.when(gives)
    def _():
        ahead().wait_send()

    @pl.when(keeps)
    def _():
        for i in range(2):
            onward(i).wait_send()

    each(bands, "wait_send", 0)
    for n in range(2):
        each(corners[n], "wait_send", 0)


CHUNK = (9, 8, 7, 6, 5, 8)


def widen_kernel(smooth_in, coarse_in, smooth_out, coarse_out, wide, sems):
    first = pltpu.make_async_copy(smooth_in, smooth_out, sems.at[0])
    first.start()
    copies = []
    for i in range(coarse_in.shape[0]):
        wide[i] = coarse_in[i].astype(jnp.float32)
        copy = pltpu.make_async_copy(wide.at[i], coarse_out.at[i], sems.at[1 + i])
        copy.start()
        copies.append(copy)
    first.wait()
    for copy in copies:
        copy.wait()


def widen(smooth, coarse):
    return pl.pallas_call(
        widen_kernel,
        out_shape=(
            jax.ShapeDtypeStruct(smooth.shape, jnp.float32),
            jax.ShapeDtypeStruct(coarse.shape, jnp.float32),
        ),
        in_specs=[pl.BlockSpec(memory_space=pltpu.VMEM)] * 2,
        out_specs=[pl.BlockSpec(memory_space=pltpu.HBM)] * 2,
        scratch_shapes=[pltpu.VMEM(coarse.shape, jnp.float32), pltpu.SemaphoreType.DMA((1 + coarse.shape[0],))],
        compiler_params=pltpu.CompilerParams(vmem_limit_bytes=32 << 20),
    )(smooth, coarse)


def solution(mesh):
    n_row, n_col = mesh.shape["frow"], mesh.shape["fcol"]

    def body(right_side, noise_weight, stencils, neighbours):
        rows, cols, pix = right_side.shape
        slots = stencils.shape[0]
        ext = (rows + 2 * HALO, cols + 2 * SIDE)
        tiles = ext[0] * ext[1]
        listed = jnp.transpose(neighbours, (2, 0, 1))
        smooth, coarse = pl.pallas_call(
            functools.partial(kernel, (n_row, n_col, rows, cols, pix, slots)),
            out_shape=(
                jax.ShapeDtypeStruct((rows, cols, pix), jnp.float32),
                jax.ShapeDtypeStruct((rows // 2, cols // 2 * n_col, pix), jnp.bfloat16),
            ),
            in_specs=[pl.BlockSpec(memory_space=pl.ANY)] * 4,
            out_specs=(pl.BlockSpec(memory_space=pltpu.VMEM), pl.BlockSpec(memory_space=pltpu.VMEM)),
            scratch_shapes=[
                pltpu.VMEM(ext + (pix,), jnp.float32),
                pltpu.VMEM(ext + (pix,), jnp.float32),
                pltpu.VMEM((tiles, pix), jnp.float32),
                pltpu.VMEM((2, 3, tiles, pix), jnp.bfloat16),
                pltpu.VMEM((slots, tiles, 128), jnp.bfloat16),
                pltpu.VMEM((pix // 128, rows * ext[1], 128), jnp.float32),
                pltpu.VMEM((slots, rows, cols), jnp.int32),
                pltpu.VMEM((slots, pix, pix), jnp.bfloat16),
                pltpu.VMEM((2 * rows * cols + cols, pix), jnp.bfloat16),
                pltpu.VMEM((2, 2 * HALO * cols + cols, pix), jnp.bfloat16),
                pltpu.VMEM((2, 2 * rows * SIDE + 2 * SIDE, pix), jnp.bfloat16),
                pltpu.VMEM((2, 2 * rows * SIDE + 2 * SIDE, pix), jnp.bfloat16),
                pltpu.VMEM((4, 2 * HALO * SIDE + 2 * SIDE, pix), jnp.bfloat16),
                pltpu.VMEM((2, 2 * rows * SIDE + 2 * SIDE, pix), jnp.bfloat16),
                pltpu.SemaphoreType.DMA((4,)),
                pltpu.SemaphoreType.DMA((8,)),
                pltpu.SemaphoreType.DMA((8,)),
                pltpu.SemaphoreType.DMA((65,)),
                pltpu.SemaphoreType.DMA((65,)),
                pltpu.SemaphoreType.DMA((3,)),
                pltpu.SemaphoreType.DMA((2,)),
                pltpu.SemaphoreType.REGULAR,
                pltpu.SemaphoreType.REGULAR((2,)),
            ],
            compiler_params=pltpu.CompilerParams(
                collective_id=0, has_side_effects=True, vmem_limit_bytes=48 << 20,
            ),
        )(*[pltpu.with_memory_space_constraint(v, pltpu.HBM) for v in (right_side, noise_weight, stencils, listed)])
        return widen(smooth, coarse)

    placed = (P("frow", "fcol", None), P("frow", "fcol", None), P(), P("frow", "fcol", None))
    return jax.shard_map(
        body,
        mesh=mesh,
        in_specs=placed,
        out_specs=(P("frow", "fcol", None), P("frow", None, None)),
        check_vma=False,
    )
```

```python
import functools

import jax
import jax.numpy as jnp
from jax import lax
from jax.experimental import pallas as pl
from jax.experimental.pallas import tpu as pltpu
from jax.sharding import PartitionSpec as P

MESH = pl.DeviceIdType.MESH
LOWER, UPPER, DEG, SWEEPS = 1.5, 6.0, 3, 2
HALO = DEG * SWEEPS
SIDE = 8
MIDDLE = 3.75


def coefficients():
    center = 0.5 * (UPPER + LOWER)
    half_width = 0.5 * (UPPER - LOWER)
    spread = center / half_width
    steps = []
    for _ in range(SWEEPS):
        ratio = 1.0 / spread
        for step in range(DEG):
            if step < DEG - 1:
                after = 1.0 / (2.0 * spread - ratio)
                steps.append((after * ratio, 2.0 * after / half_width))
                ratio = after
            else:
                steps.append((0.0, 1.0 / center))
    return center, steps


def kernel(
    sizes, rs, nw, st, nb, sol_ref, out_ref, res, wgt, drc, dir_bf, msk, fin, own_nb, stv,
    band_out, band_in, strip_out, strip_in, corner_in, side_mask, loc_sem, h_send, h_recv, g_send, g_recv
):
    n_row, n_col, rows, cols, pix, slots = sizes
    ext_rows, ext_cols = rows + 2 * HALO, cols + 2 * SIDE
    frow, fcol = lax.axis_index("frow"), lax.axis_index("fcol")
    f32, bf16 = jnp.float32, jnp.bfloat16
    has = {"up": frow > 0, "down": frow < n_row - 1, "left": fcol > 0, "right": fcol < n_col - 1}
    beside = {"up": (frow - 1, fcol), "down": (frow + 1, fcol), "left": (frow, fcol - 1), "right": (frow, fcol + 1)}
    sides = ("up", "down", "left", "right")
    y, zh = lax.rem(fcol, 4), lax.rem(fcol // 4, 2)

    def along_x(d):
        return lax.rem(fcol + 8 * d, n_col)

    def along_y(d):
        return fcol - y + lax.rem(y + d, 4)

    partner = fcol + 4 - 8 * zh
    away = {"left": jnp.logical_and(y == 0, has["left"]), "right": jnp.logical_and(y == 3, has["right"])}
    far = jnp.logical_or(away["left"], away["right"])
    far_left = y == 0
    far_side = jnp.where(far_left, 0, 1)

    barrier = pltpu.get_barrier_semaphore()
    for side in sides:

        @pl.when(has[side])
        def _(side=side):
            pl.semaphore_signal(barrier, inc=1, device_id=beside[side], device_id_type=MESH)

    for peer in [along_x(d) for d in (1, 2, 3)] + [along_y(d) for d in (1, 2, 3)] + [partner]:
        pl.semaphore_signal(barrier, inc=1, device_id=(frow, peer), device_id_type=MESH)

    local = [
        pltpu.make_async_copy(nb, own_nb, loc_sem.at[0]),
        pltpu.make_async_copy(rs, res.at[pl.ds(HALO, rows), pl.ds(SIDE, cols)], loc_sem.at[1]),
        pltpu.make_async_copy(nw, wgt.at[pl.ds(HALO, rows), pl.ds(SIDE, cols)], loc_sem.at[2]),
        pltpu.make_async_copy(st, stv, loc_sem.at[3]),
    ]
    for copy in local:
        copy.start()

    for n, side in enumerate(("up", "down")):

        @pl.when(jnp.logical_not(has[side]))
        def _(n=n):
            band_in[n] = jnp.zeros(band_in.shape[1:], bf16)
            corner_in[2 * n] = jnp.zeros(corner_in.shape[1:], bf16)
            corner_in[2 * n + 1] = jnp.zeros(corner_in.shape[1:], bf16)

    for n, side in enumerate(("left", "right")):

        @pl.when(jnp.logical_not(has[side]))
        def _(n=n):
            strip_in[n] = jnp.zeros(strip_in.shape[1:], bf16)

    for copy in local[:3]:
        copy.wait()
    flat = jnp.where(own_nb[...] >= 0, 1.0, 0.0).astype(f32).reshape(slots * rows, cols)
    flat = jnp.concatenate([flat, jnp.zeros((128 - slots * rows, cols), f32)], axis=0)
    turned = jnp.transpose(flat)
    listed = jnp.concatenate([turned, jnp.zeros((cols, pix - 128), f32)], axis=1)
    half = rows // 2 - 1
    unit, small = 2 * cols, 2 * SIDE

    def spot(row, size, middle):
        return row * size + (middle if row >= half else 0)

    for n, c0 in ((0, 0), (1, cols - SIDE)):
        strip_out[n, pl.ds(half * small, small), :] = jnp.concatenate(
            [listed[c0 : c0 + SIDE], jnp.zeros((SIDE, pix), f32)], axis=0
        ).astype(bf16)
    for row in range(rows):
        for n, c0 in ((0, 0), (1, cols - SIDE)):
            strip_out[n, pl.ds(spot(row, small, small), small), :] = jnp.concatenate(
                [
                    res[HALO + row, pl.ds(SIDE + c0, SIDE), :],
                    wgt[HALO + row, pl.ds(SIDE + c0, SIDE), :] - MIDDLE,
                ],
                axis=0,
            ).astype(bf16)

    band_size = HALO * unit + cols
    corner_size = HALO * small + small

    def remote(src, dst, index, peer):
        return pltpu.make_async_remote_copy(
            src_ref=src, dst_ref=dst, send_sem=h_send.at[index], recv_sem=h_recv.at[index],
            device_id=peer, device_id_type=MESH,
        )

    far_band, far_strip = pl.ds((rows - HALO) * unit, band_size), pl.ds((rows - HALO) * small, corner_size)
    near_band, near_strip = pl.ds(0, band_size), pl.ds(0, corner_size)
    strips = [
        ("right", "left", lambda: remote(strip_out.at[1], strip_in.at[0], 0, beside["right"])),
        ("left", "right", lambda: remote(strip_out.at[0], strip_in.at[1], 1, beside["left"])),
    ]
    bands = [
        ("down", "up", lambda: remote(band_out.at[far_band], band_in.at[0], 2, beside["down"])),
        ("up", "down", lambda: remote(band_out.at[near_band], band_in.at[1], 3, beside["up"])),
    ]
    corners = [
        [
            ("down", "up", lambda n=n: remote(strip_in.at[n, far_strip], corner_in.at[n], 4 + n, beside["down"])),
            ("up", "down", lambda n=n: remote(strip_in.at[n, near_strip], corner_in.at[2 + n], 6 + n, beside["up"])),
        ]
        for n in range(2)
    ]

    def each(copies, act, by):
        for entry in copies:

            @pl.when(has[entry[by]])
            def _(entry=entry):
                getattr(entry[2](), act)()

    amount = 7
    for side in sides:
        amount = amount + jnp.where(has[side], 1, 0)
    pl.semaphore_wait(barrier, amount)
    each(strips, "start", 0)
    band_out[pl.ds(half * unit, cols), :] = listed.astype(bf16)
    for row in range(rows):
        r = res[HALO + row, pl.ds(SIDE, cols), :]
        w = wgt[HALO + row, pl.ds(SIDE, cols), :] - MIDDLE
        band_out[pl.ds(spot(row, unit, cols), unit), :] = jnp.concatenate([r, w], axis=0).astype(bf16)
    each(bands, "start", 0)

    def mask_rows(first, last, base, left, middle, right):
        whole = jnp.concatenate([left, middle, right], axis=0)
        for k in range(slots):
            for row in range(first, last):
                m = k * rows + row
                wide = jnp.broadcast_to(whole[:, m : m + 1], (ext_cols, 128)).astype(bf16)
                msk[k, pl.ds((base + row - first) * ext_cols, ext_cols), :] = wide

    for n, side in enumerate(("left", "right")):

        @pl.when(jnp.logical_not(away[side]))
        def _(n=n):
            each(strips[n : n + 1], "wait_recv", 1)
            each(corners[n], "start", 0)

    for m, side, c0 in ((0, "left", 0), (1, "right", SIDE + cols)):

        @pl.when(jnp.logical_not(away[side]))
        def _(m=m, c0=c0):
            for row in range(rows):
                part = strip_in[m, pl.ds(spot(row, small, small), small), :].astype(f32)
                res[HALO + row, pl.ds(c0, SIDE), :] = part[:SIDE]
                wgt[HALO + row, pl.ds(c0, SIDE), :] = part[SIDE:] + MIDDLE
            side_mask[m] = strip_in[m, pl.ds(half * small, small), :].astype(f32)[:SIDE, :128]

        @pl.when(away[side])
        def _(m=m, c0=c0):
            res[:, pl.ds(c0, SIDE), :] = jnp.zeros((ext_rows, SIDE, pix), f32)
            wgt[:, pl.ds(c0, SIDE), :] = jnp.zeros((ext_rows, SIDE, pix), f32)
            for n in range(3):
                side_mask[2 * n + m] = jnp.zeros((SIDE, 128), f32)

    mask_rows(0, rows, HALO, side_mask[0], turned, side_mask[1])
    each(bands, "wait_recv", 1)
    both = ((0, 0, rows - HALO), (1, HALO + rows, 0))
    for n, base, skip in both:
        for i in range(HALO):
            part = band_in[n, pl.ds(spot(i + skip, unit, cols) - skip * unit, unit), :].astype(f32)
            res[base + i, pl.ds(SIDE, cols), :] = part[:cols]
            wgt[base + i, pl.ds(SIDE, cols), :] = part[cols:] + MIDDLE
    for n, side in enumerate(("left", "right")):

        @pl.when(jnp.logical_not(away[side]))
        def _(n=n):
            each(corners[n], "wait_recv", 1)

    for n, base, skip in both:
        offset = half - skip
        for m, side, c0 in ((0, "left", 0), (1, "right", SIDE + cols)):

            @pl.when(jnp.logical_not(away[side]))
            def _(m=m, c0=c0, n=n, base=base, skip=skip, offset=offset):
                for i in range(HALO):
                    at = pl.ds(spot(i + skip, small, small) - skip * small, small)
                    part = corner_in[2 * n + m, at, :].astype(f32)
                    res[base + i, pl.ds(c0, SIDE), :] = part[:SIDE]
                    wgt[base + i, pl.ds(c0, SIDE), :] = part[SIDE:] + MIDDLE
                side_mask[2 + 2 * n + m] = corner_in[2 * n + m, pl.ds(offset * small, small), :].astype(f32)[:SIDE, :128]

        mask_rows(
            skip, skip + HALO, base, side_mask[2 + 2 * n],
            band_in[n, pl.ds(offset * unit, cols), :].astype(f32)[:, :128], side_mask[3 + 2 * n],
        )
    local[3].wait()

    center, steps = coefficients()

    def put(buf, t0, count, value):
        for j, shift in enumerate((1, 0, count - 1)):
            moved = value if shift == 0 else pltpu.roll(value, shift, axis=0)
            dir_bf[buf, j, pl.ds(t0, count), :] = moved.astype(jnp.bfloat16)

    res_flat = res.reshape(ext_rows * ext_cols, pix)
    wgt_flat = wgt.reshape(ext_rows * ext_cols, pix)

    def begin(i, c):
        t0 = pl.multiple_of(i * (2 * ext_cols), 2 * ext_cols)
        d = res_flat[pl.ds(t0, 2 * ext_cols), :] * (1.0 / center)
        drc[pl.ds(t0, 2 * ext_cols), :] = d
        put(0, t0, 2 * ext_cols, d)
        return c

    lax.fori_loop(0, ext_rows // 2, begin, 0)

    drc_cube = drc.reshape(ext_rows, ext_cols, pix)

    for op in range(HALO):
        now, later = op, op + 1
        low = op + 1
        count = ext_rows - 2 * low
        chunk = CHUNK[op]
        size = chunk * ext_cols
        low_col = jnp.where(away["left"], SIDE + op, 0)
        high_col = jnp.where(away["right"], SIDE + cols - op, ext_cols)
        own = drc_cube[pl.ds(HALO, rows), pl.ds(SIDE, cols), :]
        at_col = lax.broadcasted_iota(jnp.int32, (rows, cols, pix), 1) + SIDE
        own = jnp.where(jnp.logical_and(at_col >= low_col, at_col < high_col), own, 0.0)
        sol_ref[...] = own if op == 0 else sol_ref[...] + own

        def apply(i, c, now=now, later=later, low=low, size=size, op=op, low_col=low_col, high_col=high_col):
            t0 = pl.multiple_of(low * ext_cols + i * size, ext_cols)
            parts = []
            for k in range(slots):
                src = t0 + (k // 3 - 1) * ext_cols
                part = dir_bf[now, k % 3, pl.ds(pl.multiple_of(src, ext_cols), size), :]
                keep = msk[k, pl.ds(t0, size), :]
                parts.append(part * jnp.concatenate([keep, keep], axis=1))
            coupled = jnp.dot(
                jnp.concatenate(parts, axis=1), stv[...].reshape(slots * pix, pix), preferred_element_type=jnp.float32
            )
            d = drc[pl.ds(t0, size), :]
            old_r = res_flat[pl.ds(t0, size), :]
            r = old_r - (wgt_flat[pl.ds(t0, size), :] * d + coupled)
            col = lax.broadcasted_iota(jnp.int32, (size // ext_cols, ext_cols, pix), 1).reshape(size, pix)
            exact = jnp.logical_and(col > low_col, col < high_col - 1)
            if op == HALO - 1:
                for h in range(pix // 128):
                    fin[h] = r[:, h * 128 : (h + 1) * 128]
            else:
                res_flat[pl.ds(t0, size), :] = jnp.where(exact, r, old_r)
                old, new = steps[op]
                after = new * r if old == 0.0 else old * d + new * r
                drc[pl.ds(t0, size), :] = jnp.where(exact, after, d)
                put(later, t0, size, after)
            return c

        trips = count // chunk
        if trips == 1:
            apply(0, 0)
        else:
            lax.fori_loop(0, trips, apply, 0)
        if op == AWAIT:
            for n, side in enumerate(("left", "right")):

                @pl.when(away[side])
                def _(n=n):
                    each(strips[n : n + 1], "wait_recv", 1)
                    each(corners[n], "start", 0)

    @pl.when(far)
    def _():
        for n, side in enumerate(("left", "right")):

            @pl.when(away[side])
            def _(n=n):
                each(corners[n], "wait_recv", 1)

        width = 2 * SIDE
        c0 = pl.multiple_of(jnp.where(far_left, 0, ext_cols - width), width)
        outer = pl.ds(pl.multiple_of(jnp.where(far_left, 0, ext_cols - SIDE), SIDE), SIDE)
        for row in range(rows):
            part = strip_in[far_side, pl.ds(spot(row, small, small), small), :].astype(f32)
            res[HALO + row, outer, :] = part[:SIDE]
            wgt[HALO + row, outer, :] = part[SIDE:] + MIDDLE
        for n, base, skip in both:
            for i in range(HALO):
                at = pl.ds(spot(i + skip, small, small) - skip * small, small)
                part = corner_in[2 * n + far_side, at, :].astype(f32)
                res[base + i, outer, :] = part[:SIDE]
                wgt[base + i, outer, :] = part[SIDE:] + MIDDLE

        def window_masks(start, stop, base, halo, inner):
            halo = halo.astype(f32)[:SIDE, :128]
            whole = jnp.where(
                far_left,
                jnp.concatenate([halo, inner[:SIDE]], axis=0),
                jnp.concatenate([inner[cols - SIDE :], halo], axis=0),
            )
            for k in range(slots):
                for row in range(start, stop):
                    m = k * rows + row
                    wide = jnp.broadcast_to(whole[:, m : m + 1], (width, 128)).astype(bf16)
                    msk[k, pl.ds(pl.multiple_of((base + row - start) * ext_cols + c0, width), width), :] = wide

        window_masks(0, rows, HALO, strip_in[far_side, pl.ds(half * small, small), :], turned)
        for n, base, skip in both:
            offset = half - skip
            window_masks(
                skip, skip + HALO, base, corner_in[2 * n + far_side, pl.ds(offset * small, small), :],
                band_in[n, pl.ds(offset * unit, cols), :].astype(f32)[:, :128],
            )

        res_cube, dir_cube = res, dir_bf.reshape(HALO, 3, ext_rows, ext_cols, pix)
        msk_cube = msk.reshape(slots, ext_rows, ext_cols, 128)
        span = pl.ds(c0, width)

        def edges(count):
            inside = lax.broadcasted_iota(jnp.int32, (count, width, pix), 1).reshape(count * width, pix)
            return inside, jnp.where(far_left, inside, width - 1 - inside)

        def put_window(level, first, count, value):
            at = pl.ds(first, count)
            inside, edge = edges(count)

            def held(j):
                return dir_cube[level, j, at, span, :].reshape(count * width, pix).astype(f32)

            value = jnp.where(edge < SIDE + level, value, held(1))
            back = jnp.where(inside == 0, held(0), pltpu.roll(value, 1, axis=0))
            ahead = jnp.where(inside == width - 1, held(2), pltpu.roll(value, count * width - 1, axis=0))
            for j, moved in enumerate((back, value, ahead)):
                dir_cube[level, j, at, span, :] = moved.astype(bf16).reshape(count, width, pix)

        def get(cube, first, count):
            return cube[pl.ds(first, count), span, :].reshape(count * width, pix)

        start = get(res_cube, 0, ext_rows) * (1.0 / center)
        _, edge = edges(ext_rows)
        start = jnp.where(edge < SIDE, start, get(drc_cube, 0, ext_rows))
        drc_cube[:, span, :] = start.reshape(ext_rows, width, pix)
        put_window(0, 0, ext_rows, start)
        inner_span = pl.ds(pl.multiple_of(jnp.where(far_left, SIDE, ext_cols - width), SIDE), SIDE)
        sol_span = pl.ds(pl.multiple_of(jnp.where(far_left, 0, cols - SIDE), SIDE), SIDE)
        within = lax.broadcasted_iota(jnp.int32, (rows, SIDE, pix), 1)
        within = jnp.where(far_left, within, SIDE - 1 - within)
        for op in range(HALO):
            low = op + 1
            count = ext_rows - 2 * low
            if op > 0:
                more = drc_cube[pl.ds(HALO, rows), inner_span, :]
                sol_ref[:, sol_span, :] = sol_ref[:, sol_span, :] + jnp.where(within < op, more, 0.0)
            parts = []
            for k in range(slots):
                part = dir_cube[op, k % 3, pl.ds(low + k // 3 - 1, count), span, :].reshape(count * width, pix)
                keep = msk_cube[k, pl.ds(low, count), span, :].reshape(count * width, 128)
                parts.append(part * jnp.concatenate([keep, keep], axis=1))
            coupled = jnp.dot(
                jnp.concatenate(parts, axis=1), stv[...].reshape(slots * pix, pix), preferred_element_type=f32
            )
            d, old_r = get(drc_cube, low, count), get(res_cube, low, count)
            r = old_r - (get(wgt, low, count) * d + coupled)
            _, edge = edges(count)
            exact = edge < SIDE + low
            if op == HALO - 1:
                for h in range(pix // 128):
                    fin_cube = fin.reshape(pix // 128, rows, ext_cols, 128)
                    was = fin_cube[h, :, span, :].reshape(count * width, 128)
                    now = jnp.where(exact[:, :128], r[:, h * 128 : (h + 1) * 128], was)
                    fin_cube[h, :, span, :] = now.reshape(count, width, 128)
            else:
                old, new = steps[op]
                after = new * r if old == 0.0 else old * d + new * r
                res_cube[pl.ds(low, count), span, :] = jnp.where(exact, r, old_r).reshape(count, width, pix)
                drc_cube[pl.ds(low, count), span, :] = jnp.where(exact, after, d).reshape(count, width, pix)
                put_window(low, low, count, after)

    pixel = lax.broadcasted_iota(jnp.int32, (pix, 128), 0)
    lane = lax.broadcasted_iota(jnp.int32, (pix, 128), 1)
    fold = jnp.where(pixel // 4 == lane % 64, 1.0, 0.0).astype(jnp.bfloat16)
    pieces = []
    for a in range(2):
        for b in range(2):
            for R in range(rows // 2):
                begin_at = (2 * R + a) * ext_cols + SIDE + b
                pieces.append(
                    jnp.concatenate(
                        [fin[h, pl.ds(begin_at, cols // 2, stride=2), :] for h in range(pix // 128)], axis=1
                    )
                )
    stack = jnp.concatenate(pieces, axis=0)
    high = stack.astype(jnp.bfloat16)
    low_part = (stack - high.astype(jnp.float32)).astype(jnp.bfloat16)
    summed = jnp.dot(high, fold, preferred_element_type=jnp.float32) + jnp.dot(
        low_part, fold, preferred_element_type=jnp.float32
    )
    quarter = (rows // 2) * (cols // 2)
    quads = [summed[q * quarter : (q + 1) * quarter] for q in range(4)]
    left = lax.broadcasted_iota(jnp.int32, (quarter, 128), 1) < 64
    coarse = jnp.concatenate([jnp.where(left, quads[0], quads[1]), jnp.where(left, quads[2], quads[3])], axis=1).astype(jnp.bfloat16)
    quarter_cols = cols // 2
    group = rows // 4

    def block(j, half=None):
        span = pl.ds(pl.multiple_of(j * quarter_cols, quarter_cols), quarter_cols)
        if half is None:
            return out_ref.at[:, span, :]
        return out_ref.at[pl.ds(half * group, group), span, :]

    out_ref[:, pl.ds(pl.multiple_of(fcol * quarter_cols, quarter_cols), quarter_cols), :] = coarse.reshape(
        rows // 2, quarter_cols, pix
    )

    def move(ref, index, peer):
        return pltpu.make_async_remote_copy(
            src_ref=ref, dst_ref=ref, send_sem=g_send.at[index], recv_sem=g_recv.at[index],
            device_id=(frow, peer), device_id_type=MESH,
        )

    routes = ((along_x, along_y), (along_y, along_x))

    def source(way, d, which):
        return way((4 - d) % 4) + which * (4 - 8 * zh)

    def index_of(which, half, d1, d2):
        return 1 + ((which * 2 + half) * 4 + d1) * 4 + d2

    sent = [move(block(fcol), 0, partner)]
    sent[0].start()
    near = (1, 3, 2)
    for which in range(2):
        base = fcol + which * (4 - 8 * zh)
        if which == 1:
            move(block(base), 0, partner).wait_recv()
        for stage in range(2):
            for half in range(2):
                for d in near:
                    key = index_of(which, half, d, 0) if stage == 0 else index_of(which, half, 0, d)
                    copy = move(block(base, half), key, routes[half][stage](d))
                    copy.start()
                    sent.append(copy)
        for d1 in near:
            for half in range(2):
                ref = block(source(routes[half][0], d1, which), half)
                move(ref, index_of(which, half, d1, 0), fcol).wait_recv()
                for d2 in near:
                    copy = move(ref, index_of(which, half, d1, d2), routes[half][1](d2))
                    copy.start()
                    sent.append(copy)
    for which in range(2):
        for half in range(2):
            for d1 in (0,) + near:
                for d2 in near:
                    move(block(fcol, half), index_of(which, half, d1, d2), fcol).wait_recv()
    for copy in sent:
        copy.wait_send()
    each(strips, "wait_send", 0)
    each(bands, "wait_send", 0)
    for n in range(2):
        each(corners[n], "wait_send", 0)


AWAIT = 2
CHUNK = (9, 8, 7, 6, 5, 8)


def widen_kernel(smooth_in, coarse_in, smooth_out, coarse_out, wide, sems):
    first = pltpu.make_async_copy(smooth_in, smooth_out, sems.at[0])
    first.start()
    copies = []
    for i in range(coarse_in.shape[0]):
        wide[i] = coarse_in[i].astype(jnp.float32)
        copy = pltpu.make_async_copy(wide.at[i], coarse_out.at[i], sems.at[1 + i])
        copy.start()
        copies.append(copy)
    first.wait()
    for copy in copies:
        copy.wait()


def widen(smooth, coarse):
    return pl.pallas_call(
        widen_kernel,
        out_shape=(
            jax.ShapeDtypeStruct(smooth.shape, jnp.float32),
            jax.ShapeDtypeStruct(coarse.shape, jnp.float32),
        ),
        in_specs=[pl.BlockSpec(memory_space=pltpu.VMEM)] * 2,
        out_specs=[pl.BlockSpec(memory_space=pltpu.HBM)] * 2,
        scratch_shapes=[pltpu.VMEM(coarse.shape, jnp.float32), pltpu.SemaphoreType.DMA((1 + coarse.shape[0],))],
        compiler_params=pltpu.CompilerParams(vmem_limit_bytes=32 << 20),
    )(smooth, coarse)


def solution(mesh):
    n_row, n_col = mesh.shape["frow"], mesh.shape["fcol"]

    def body(right_side, noise_weight, stencils, neighbours):
        rows, cols, pix = right_side.shape
        slots = stencils.shape[0]
        ext = (rows + 2 * HALO, cols + 2 * SIDE)
        tiles = ext[0] * ext[1]
        listed = jnp.transpose(neighbours, (2, 0, 1))
        smooth, coarse = pl.pallas_call(
            functools.partial(kernel, (n_row, n_col, rows, cols, pix, slots)),
            out_shape=(
                jax.ShapeDtypeStruct((rows, cols, pix), jnp.float32),
                jax.ShapeDtypeStruct((rows // 2, cols // 2 * n_col, pix), jnp.bfloat16),
            ),
            in_specs=[pl.BlockSpec(memory_space=pl.ANY)] * 4,
            out_specs=(pl.BlockSpec(memory_space=pltpu.VMEM), pl.BlockSpec(memory_space=pltpu.VMEM)),
            scratch_shapes=[
                pltpu.VMEM(ext + (pix,), jnp.float32),
                pltpu.VMEM(ext + (pix,), jnp.float32),
                pltpu.VMEM((tiles, pix), jnp.float32),
                pltpu.VMEM((HALO, 3, tiles, pix), jnp.bfloat16),
                pltpu.VMEM((slots, tiles, 128), jnp.bfloat16),
                pltpu.VMEM((pix // 128, rows * ext[1], 128), jnp.float32),
                pltpu.VMEM((slots, rows, cols), jnp.int32),
                pltpu.VMEM((slots, pix, pix), jnp.bfloat16),
                pltpu.VMEM((2 * rows * cols + cols, pix), jnp.bfloat16),
                pltpu.VMEM((2, 2 * HALO * cols + cols, pix), jnp.bfloat16),
                pltpu.VMEM((2, 2 * rows * SIDE + 2 * SIDE, pix), jnp.bfloat16),
                pltpu.VMEM((2, 2 * rows * SIDE + 2 * SIDE, pix), jnp.bfloat16),
                pltpu.VMEM((4, 2 * HALO * SIDE + 2 * SIDE, pix), jnp.bfloat16),
                pltpu.VMEM((6, SIDE, 128), jnp.float32),
                pltpu.SemaphoreType.DMA((4,)),
                pltpu.SemaphoreType.DMA((8,)),
                pltpu.SemaphoreType.DMA((8,)),
                pltpu.SemaphoreType.DMA((65,)),
                pltpu.SemaphoreType.DMA((65,)),
            ],
            compiler_params=pltpu.CompilerParams(
                collective_id=0, has_side_effects=True, vmem_limit_bytes=48 << 20,
            ),
        )(*[pltpu.with_memory_space_constraint(v, pltpu.HBM) for v in (right_side, noise_weight, stencils, listed)])
        return widen(smooth, coarse)

    placed = (P("frow", "fcol", None), P("frow", "fcol", None), P(), P("frow", "fcol", None))
    return jax.shard_map(
        body,
        mesh=mesh,
        in_specs=placed,
        out_specs=(P("frow", "fcol", None), P("frow", None, None)),
        check_vma=False,
    )
```

```python
import functools

import jax
import jax.numpy as jnp
from jax import lax
from jax.experimental import pallas as pl
from jax.experimental.pallas import tpu as pltpu
from jax.sharding import PartitionSpec as P

MESH = pl.DeviceIdType.MESH
LOWER, UPPER, DEG, SWEEPS = 1.5, 6.0, 3, 2
HALO = DEG * SWEEPS
SIDE = 8
MIDDLE = 3.75


def coefficients():
    center = 0.5 * (UPPER + LOWER)
    half_width = 0.5 * (UPPER - LOWER)
    spread = center / half_width
    steps = []
    for _ in range(SWEEPS):
        ratio = 1.0 / spread
        for step in range(DEG):
            if step < DEG - 1:
                after = 1.0 / (2.0 * spread - ratio)
                steps.append((after * ratio, 2.0 * after / half_width))
                ratio = after
            else:
                steps.append((0.0, 1.0 / center))
    return center, steps


def kernel(
    sizes, rs, nw, st, nb, sol_ref, out_ref, res, wgt, drc, dir_bf, msk, fin, own_nb, stv,
    band_out, band_in, strip_out, strip_in, corner_in, side_mask, loc_sem, h_send, h_recv, g_send, g_recv
):
    n_row, n_col, rows, cols, pix, slots = sizes
    ext_rows, ext_cols = rows + 2 * HALO, cols + 2 * SIDE
    frow, fcol = lax.axis_index("frow"), lax.axis_index("fcol")
    f32, bf16 = jnp.float32, jnp.bfloat16
    has = {"up": frow > 0, "down": frow < n_row - 1, "left": fcol > 0, "right": fcol < n_col - 1}
    beside = {"up": (frow - 1, fcol), "down": (frow + 1, fcol), "left": (frow, fcol - 1), "right": (frow, fcol + 1)}
    sides = ("up", "down", "left", "right")
    y, zh = lax.rem(fcol, 4), lax.rem(fcol // 4, 2)

    def along_x(d):
        return lax.rem(fcol + 8 * d, n_col)

    def along_y(d):
        return fcol - y + lax.rem(y + d, 4)

    partner = fcol + 4 - 8 * zh
    away = {"left": jnp.logical_and(y == 0, has["left"]), "right": jnp.logical_and(y == 3, has["right"])}
    far = jnp.logical_or(away["left"], away["right"])
    far_left = y == 0
    far_side = jnp.where(far_left, 0, 1)

    barrier = pltpu.get_barrier_semaphore()
    for side in sides:

        @pl.when(has[side])
        def _(side=side):
            pl.semaphore_signal(barrier, inc=1, device_id=beside[side], device_id_type=MESH)

    for peer in [along_x(d) for d in (1, 2, 3)] + [along_y(d) for d in (1, 2, 3)] + [partner]:
        pl.semaphore_signal(barrier, inc=1, device_id=(frow, peer), device_id_type=MESH)

    local = [
        pltpu.make_async_copy(nb, own_nb, loc_sem.at[0]),
        pltpu.make_async_copy(rs, res.at[pl.ds(HALO, rows), pl.ds(SIDE, cols)], loc_sem.at[1]),
        pltpu.make_async_copy(nw, wgt.at[pl.ds(HALO, rows), pl.ds(SIDE, cols)], loc_sem.at[2]),
        pltpu.make_async_copy(st, stv, loc_sem.at[3]),
    ]
    for copy in local:
        copy.start()

    for n, side in enumerate(("up", "down")):

        @pl.when(jnp.logical_not(has[side]))
        def _(n=n):
            band_in[n] = jnp.zeros(band_in.shape[1:], bf16)
            corner_in[2 * n] = jnp.zeros(corner_in.shape[1:], bf16)
            corner_in[2 * n + 1] = jnp.zeros(corner_in.shape[1:], bf16)

    for n, side in enumerate(("left", "right")):

        @pl.when(jnp.logical_not(has[side]))
        def _(n=n):
            strip_in[n] = jnp.zeros(strip_in.shape[1:], bf16)

    for copy in local[:3]:
        copy.wait()
    flat = jnp.where(own_nb[...] >= 0, 1.0, 0.0).astype(f32).reshape(slots * rows, cols)
    flat = jnp.concatenate([flat, jnp.zeros((128 - slots * rows, cols), f32)], axis=0)
    turned = jnp.transpose(flat)
    listed = jnp.concatenate([turned, jnp.zeros((cols, pix - 128), f32)], axis=1)
    half = rows // 2 - 1
    unit, small = 2 * cols, 2 * SIDE

    def spot(row, size, middle):
        return row * size + (middle if row >= half else 0)

    for n, c0 in ((0, 0), (1, cols - SIDE)):
        strip_out[n, pl.ds(half * small, small), :] = jnp.concatenate(
            [listed[c0 : c0 + SIDE], jnp.zeros((SIDE, pix), f32)], axis=0
        ).astype(bf16)
    for row in range(rows):
        for n, c0 in ((0, 0), (1, cols - SIDE)):
            strip_out[n, pl.ds(spot(row, small, small), small), :] = jnp.concatenate(
                [
                    res[HALO + row, pl.ds(SIDE + c0, SIDE), :],
                    wgt[HALO + row, pl.ds(SIDE + c0, SIDE), :] - MIDDLE,
                ],
                axis=0,
            ).astype(bf16)

    band_size = HALO * unit + cols
    corner_size = HALO * small + small

    def remote(src, dst, index, peer):
        return pltpu.make_async_remote_copy(
            src_ref=src, dst_ref=dst, send_sem=h_send.at[index], recv_sem=h_recv.at[index],
            device_id=peer, device_id_type=MESH,
        )

    far_band, far_strip = pl.ds((rows - HALO) * unit, band_size), pl.ds((rows - HALO) * small, corner_size)
    near_band, near_strip = pl.ds(0, band_size), pl.ds(0, corner_size)
    strips = [
        ("right", "left", lambda: remote(strip_out.at[1], strip_in.at[0], 0, beside["right"])),
        ("left", "right", lambda: remote(strip_out.at[0], strip_in.at[1], 1, beside["left"])),
    ]
    bands = [
        ("down", "up", lambda: remote(band_out.at[far_band], band_in.at[0], 2, beside["down"])),
        ("up", "down", lambda: remote(band_out.at[near_band], band_in.at[1], 3, beside["up"])),
    ]
    corners = [
        [
            ("down", "up", lambda n=n: remote(strip_in.at[n, far_strip], corner_in.at[n], 4 + n, beside["down"])),
            ("up", "down", lambda n=n: remote(strip_in.at[n, near_strip], corner_in.at[2 + n], 6 + n, beside["up"])),
        ]
        for n in range(2)
    ]

    def each(copies, act, by):
        for entry in copies:

            @pl.when(has[entry[by]])
            def _(entry=entry):
                getattr(entry[2](), act)()

    amount = 7
    for side in sides:
        amount = amount + jnp.where(has[side], 1, 0)
    pl.semaphore_wait(barrier, amount)
    each(strips, "start", 0)
    band_out[pl.ds(half * unit, cols), :] = listed.astype(bf16)
    for row in range(rows):
        r = res[HALO + row, pl.ds(SIDE, cols), :]
        w = wgt[HALO + row, pl.ds(SIDE, cols), :] - MIDDLE
        band_out[pl.ds(spot(row, unit, cols), unit), :] = jnp.concatenate([r, w], axis=0).astype(bf16)
    each(bands, "start", 0)

    def mask_rows(first, last, base, left, middle, right):
        whole = jnp.concatenate([left, middle, right], axis=0)
        for k in range(slots):
            for row in range(first, last):
                m = k * rows + row
                wide = jnp.broadcast_to(whole[:, m : m + 1], (ext_cols, 128)).astype(bf16)
                msk[k, pl.ds((base + row - first) * ext_cols, ext_cols), :] = wide

    for n, side in enumerate(("left", "right")):

        @pl.when(jnp.logical_not(away[side]))
        def _(n=n):
            each(strips[n : n + 1], "wait_recv", 1)
            each(corners[n], "start", 0)

    for m, side, c0 in ((0, "left", 0), (1, "right", SIDE + cols)):

        @pl.when(jnp.logical_not(away[side]))
        def _(m=m, c0=c0):
            for row in range(rows):
                part = strip_in[m, pl.ds(spot(row, small, small), small), :].astype(f32)
                res[HALO + row, pl.ds(c0, SIDE), :] = part[:SIDE]
                wgt[HALO + row, pl.ds(c0, SIDE), :] = part[SIDE:] + MIDDLE
            side_mask[m] = strip_in[m, pl.ds(half * small, small), :].astype(f32)[:SIDE, :128]

        @pl.when(away[side])
        def _(m=m, c0=c0):
            res[:, pl.ds(c0, SIDE), :] = jnp.zeros((ext_rows, SIDE, pix), f32)
            wgt[:, pl.ds(c0, SIDE), :] = jnp.zeros((ext_rows, SIDE, pix), f32)
            for n in range(3):
                side_mask[2 * n + m] = jnp.zeros((SIDE, 128), f32)

    mask_rows(0, rows, HALO, side_mask[0], turned, side_mask[1])
    each(bands, "wait_recv", 1)
    both = ((0, 0, rows - HALO), (1, HALO + rows, 0))
    for n, base, skip in both:
        for i in range(HALO):
            part = band_in[n, pl.ds(spot(i + skip, unit, cols) - skip * unit, unit), :].astype(f32)
            res[base + i, pl.ds(SIDE, cols), :] = part[:cols]
            wgt[base + i, pl.ds(SIDE, cols), :] = part[cols:] + MIDDLE
    for n, side in enumerate(("left", "right")):

        @pl.when(jnp.logical_not(away[side]))
        def _(n=n):
            each(corners[n], "wait_recv", 1)

    for n, base, skip in both:
        offset = half - skip
        for m, side, c0 in ((0, "left", 0), (1, "right", SIDE + cols)):

            @pl.when(jnp.logical_not(away[side]))
            def _(m=m, c0=c0, n=n, base=base, skip=skip, offset=offset):
                for i in range(HALO):
                    at = pl.ds(spot(i + skip, small, small) - skip * small, small)
                    part = corner_in[2 * n + m, at, :].astype(f32)
                    res[base + i, pl.ds(c0, SIDE), :] = part[:SIDE]
                    wgt[base + i, pl.ds(c0, SIDE), :] = part[SIDE:] + MIDDLE
                side_mask[2 + 2 * n + m] = corner_in[2 * n + m, pl.ds(offset * small, small), :].astype(f32)[:SIDE, :128]

        mask_rows(
            skip, skip + HALO, base, side_mask[2 + 2 * n],
            band_in[n, pl.ds(offset * unit, cols), :].astype(f32)[:, :128], side_mask[3 + 2 * n],
        )
    local[3].wait()

    center, steps = coefficients()

    def put(buf, t0, count, value):
        for j, shift in enumerate((1, 0, count - 1)):
            moved = value if shift == 0 else pltpu.roll(value, shift, axis=0)
            dir_bf[buf, j, pl.ds(t0, count), :] = moved.astype(jnp.bfloat16)

    res_flat = res.reshape(ext_rows * ext_cols, pix)
    wgt_flat = wgt.reshape(ext_rows * ext_cols, pix)

    def begin(i, c):
        t0 = pl.multiple_of(i * (2 * ext_cols), 2 * ext_cols)
        d = res_flat[pl.ds(t0, 2 * ext_cols), :] * (1.0 / center)
        drc[pl.ds(t0, 2 * ext_cols), :] = d
        put(0, t0, 2 * ext_cols, d)
        return c

    lax.fori_loop(0, ext_rows // 2, begin, 0)

    drc_cube = drc.reshape(ext_rows, ext_cols, pix)

    def redo():
        for n, side in enumerate(("left", "right")):

            @pl.when(away[side])
            def _(n=n):
                each(corners[n], "wait_recv", 1)

        width = 2 * SIDE
        c0 = pl.multiple_of(jnp.where(far_left, 0, ext_cols - width), width)
        outer = pl.ds(pl.multiple_of(jnp.where(far_left, 0, ext_cols - SIDE), SIDE), SIDE)
        for row in range(rows):
            part = strip_in[far_side, pl.ds(spot(row, small, small), small), :].astype(f32)
            res[HALO + row, outer, :] = part[:SIDE]
            wgt[HALO + row, outer, :] = part[SIDE:] + MIDDLE
        for n, base, skip in both:
            for i in range(HALO):
                at = pl.ds(spot(i + skip, small, small) - skip * small, small)
                part = corner_in[2 * n + far_side, at, :].astype(f32)
                res[base + i, outer, :] = part[:SIDE]
                wgt[base + i, outer, :] = part[SIDE:] + MIDDLE

        def window_masks(start, stop, base, halo, inner):
            halo = halo.astype(f32)[:SIDE, :128]
            whole = jnp.where(
                far_left,
                jnp.concatenate([halo, inner[:SIDE]], axis=0),
                jnp.concatenate([inner[cols - SIDE :], halo], axis=0),
            )
            for k in range(slots):
                for row in range(start, stop):
                    m = k * rows + row
                    wide = jnp.broadcast_to(whole[:, m : m + 1], (width, 128)).astype(bf16)
                    msk[k, pl.ds(pl.multiple_of((base + row - start) * ext_cols + c0, width), width), :] = wide

        window_masks(0, rows, HALO, strip_in[far_side, pl.ds(half * small, small), :], turned)
        for n, base, skip in both:
            offset = half - skip
            window_masks(
                skip, skip + HALO, base, corner_in[2 * n + far_side, pl.ds(offset * small, small), :],
                band_in[n, pl.ds(offset * unit, cols), :].astype(f32)[:, :128],
            )

        res_cube, dir_cube = res, dir_bf.reshape(HALO, 3, ext_rows, ext_cols, pix)
        msk_cube = msk.reshape(slots, ext_rows, ext_cols, 128)
        span = pl.ds(c0, width)

        def edges(count):
            inside = lax.broadcasted_iota(jnp.int32, (count, width, pix), 1).reshape(count * width, pix)
            return inside, jnp.where(far_left, inside, width - 1 - inside)

        def put_window(level, first, count, value):
            at = pl.ds(first, count)
            inside, edge = edges(count)

            def held(j):
                return dir_cube[level, j, at, span, :].reshape(count * width, pix).astype(f32)

            value = jnp.where(edge < SIDE + level, value, held(1))
            back = jnp.where(inside == 0, held(0), pltpu.roll(value, 1, axis=0))
            ahead = jnp.where(inside == width - 1, held(2), pltpu.roll(value, count * width - 1, axis=0))
            for j, moved in enumerate((back, value, ahead)):
                dir_cube[level, j, at, span, :] = moved.astype(bf16).reshape(count, width, pix)

        def get(cube, first, count):
            return cube[pl.ds(first, count), span, :].reshape(count * width, pix)

        start = get(res_cube, 0, ext_rows) * (1.0 / center)
        _, edge = edges(ext_rows)
        start = jnp.where(edge < SIDE, start, get(drc_cube, 0, ext_rows))
        drc_cube[:, span, :] = start.reshape(ext_rows, width, pix)
        put_window(0, 0, ext_rows, start)
        inner_span = pl.ds(pl.multiple_of(jnp.where(far_left, SIDE, ext_cols - width), SIDE), SIDE)
        sol_span = pl.ds(pl.multiple_of(jnp.where(far_left, 0, cols - SIDE), SIDE), SIDE)
        within = lax.broadcasted_iota(jnp.int32, (rows, SIDE, pix), 1)
        within = jnp.where(far_left, within, SIDE - 1 - within)
        for op in range(AWAIT + 1):
            low = op + 1
            count = ext_rows - 2 * low
            if op > 0:
                more = drc_cube[pl.ds(HALO, rows), inner_span, :]
                sol_ref[:, sol_span, :] = sol_ref[:, sol_span, :] + jnp.where(within < op, more, 0.0)
            parts = []
            for k in range(slots):
                part = dir_cube[op, k % 3, pl.ds(low + k // 3 - 1, count), span, :].reshape(count * width, pix)
                keep = msk_cube[k, pl.ds(low, count), span, :].reshape(count * width, 128)
                parts.append(part * jnp.concatenate([keep, keep], axis=1))
            coupled = jnp.dot(
                jnp.concatenate(parts, axis=1), stv[...].reshape(slots * pix, pix), preferred_element_type=f32
            )
            d, old_r = get(drc_cube, low, count), get(res_cube, low, count)
            r = old_r - (get(wgt, low, count) * d + coupled)
            _, edge = edges(count)
            exact = edge < SIDE + low
            old, new = steps[op]
            after = new * r if old == 0.0 else old * d + new * r
            res_cube[pl.ds(low, count), span, :] = jnp.where(exact, r, old_r).reshape(count, width, pix)
            drc_cube[pl.ds(low, count), span, :] = jnp.where(exact, after, d).reshape(count, width, pix)
            put_window(low, low, count, after)

    for op in range(HALO):
        now, later = op, op + 1
        low = op + 1
        count = ext_rows - 2 * low
        chunk = CHUNK[op]
        size = chunk * ext_cols
        low_col = jnp.where(away["left"], SIDE + op, 0) if op <= AWAIT else 0
        high_col = jnp.where(away["right"], SIDE + cols - op, ext_cols) if op <= AWAIT else ext_cols
        own = drc_cube[pl.ds(HALO, rows), pl.ds(SIDE, cols), :]
        at_col = lax.broadcasted_iota(jnp.int32, (rows, cols, pix), 1) + SIDE
        own = jnp.where(jnp.logical_and(at_col >= low_col, at_col < high_col), own, 0.0)
        sol_ref[...] = own if op == 0 else sol_ref[...] + own

        def apply(i, c, now=now, later=later, low=low, size=size, op=op, low_col=low_col, high_col=high_col):
            t0 = pl.multiple_of(low * ext_cols + i * size, ext_cols)
            parts = []
            for k in range(slots):
                src = t0 + (k // 3 - 1) * ext_cols
                part = dir_bf[now, k % 3, pl.ds(pl.multiple_of(src, ext_cols), size), :]
                keep = msk[k, pl.ds(t0, size), :]
                parts.append(part * jnp.concatenate([keep, keep], axis=1))
            coupled = jnp.dot(
                jnp.concatenate(parts, axis=1), stv[...].reshape(slots * pix, pix), preferred_element_type=jnp.float32
            )
            d = drc[pl.ds(t0, size), :]
            old_r = res_flat[pl.ds(t0, size), :]
            r = old_r - (wgt_flat[pl.ds(t0, size), :] * d + coupled)
            col = lax.broadcasted_iota(jnp.int32, (size // ext_cols, ext_cols, pix), 1).reshape(size, pix)
            exact = jnp.logical_and(col > low_col, col < high_col - 1)
            if op == HALO - 1:
                for h in range(pix // 128):
                    fin[h] = r[:, h * 128 : (h + 1) * 128]
            else:
                res_flat[pl.ds(t0, size), :] = jnp.where(exact, r, old_r)
                old, new = steps[op]
                after = new * r if old == 0.0 else old * d + new * r
                drc[pl.ds(t0, size), :] = jnp.where(exact, after, d)
                put(later, t0, size, after)
            return c

        trips = count // chunk
        if trips == 1:
            apply(0, 0)
        else:
            lax.fori_loop(0, trips, apply, 0)
        if op == ASK:
            for n, side in enumerate(("left", "right")):

                @pl.when(away[side])
                def _(n=n):
                    each(strips[n : n + 1], "wait_recv", 1)
                    each(corners[n], "start", 0)

        if op == AWAIT:
            pl.when(far)(redo)

    pixel = lax.broadcasted_iota(jnp.int32, (pix, 128), 0)
    lane = lax.broadcasted_iota(jnp.int32, (pix, 128), 1)
    fold = jnp.where(pixel // 4 == lane % 64, 1.0, 0.0).astype(jnp.bfloat16)
    pieces = []
    for a in range(2):
        for b in range(2):
            for R in range(rows // 2):
                begin_at = (2 * R + a) * ext_cols + SIDE + b
                pieces.append(
                    jnp.concatenate(
                        [fin[h, pl.ds(begin_at, cols // 2, stride=2), :] for h in range(pix // 128)], axis=1
                    )
                )
    stack = jnp.concatenate(pieces, axis=0)
    high = stack.astype(jnp.bfloat16)
    low_part = (stack - high.astype(jnp.float32)).astype(jnp.bfloat16)
    summed = jnp.dot(high, fold, preferred_element_type=jnp.float32) + jnp.dot(
        low_part, fold, preferred_element_type=jnp.float32
    )
    quarter = (rows // 2) * (cols // 2)
    quads = [summed[q * quarter : (q + 1) * quarter] for q in range(4)]
    left = lax.broadcasted_iota(jnp.int32, (quarter, 128), 1) < 64
    coarse = jnp.concatenate([jnp.where(left, quads[0], quads[1]), jnp.where(left, quads[2], quads[3])], axis=1).astype(jnp.bfloat16)
    quarter_cols = cols // 2
    group = rows // 4

    def block(j, half=None):
        span = pl.ds(pl.multiple_of(j * quarter_cols, quarter_cols), quarter_cols)
        if half is None:
            return out_ref.at[:, span, :]
        return out_ref.at[pl.ds(half * group, group), span, :]

    out_ref[:, pl.ds(pl.multiple_of(fcol * quarter_cols, quarter_cols), quarter_cols), :] = coarse.reshape(
        rows // 2, quarter_cols, pix
    )

    def move(ref, index, peer):
        return pltpu.make_async_remote_copy(
            src_ref=ref, dst_ref=ref, send_sem=g_send.at[index], recv_sem=g_recv.at[index],
            device_id=(frow, peer), device_id_type=MESH,
        )

    routes = ((along_x, along_y), (along_y, along_x))

    def source(way, d, which):
        return way((4 - d) % 4) + which * (4 - 8 * zh)

    def index_of(which, half, d1, d2):
        return 1 + ((which * 2 + half) * 4 + d1) * 4 + d2

    sent = [move(block(fcol), 0, partner)]
    sent[0].start()
    near = (1, 3, 2)
    for which in range(2):
        base = fcol + which * (4 - 8 * zh)
        if which == 1:
            move(block(base), 0, partner).wait_recv()
        for stage in range(2):
            for half in range(2):
                for d in near:
                    key = index_of(which, half, d, 0) if stage == 0 else index_of(which, half, 0, d)
                    copy = move(block(base, half), key, routes[half][stage](d))
                    copy.start()
                    sent.append(copy)
        for d1 in near:
            for half in range(2):
                ref = block(source(routes[half][0], d1, which), half)
                move(ref, index_of(which, half, d1, 0), fcol).wait_recv()
                for d2 in near:
                    copy = move(ref, index_of(which, half, d1, d2), routes[half][1](d2))
                    copy.start()
                    sent.append(copy)
    for which in range(2):
        for half in range(2):
            for d1 in (0,) + near:
                for d2 in near:
                    move(block(fcol, half), index_of(which, half, d1, d2), fcol).wait_recv()
    for copy in sent:
        copy.wait_send()
    each(strips, "wait_send", 0)
    each(bands, "wait_send", 0)
    for n in range(2):
        each(corners[n], "wait_send", 0)


ASK, AWAIT = 0, 2
CHUNK = (9, 8, 7, 6, 5, 8)


def widen_kernel(smooth_in, coarse_in, smooth_out, coarse_out, wide, sems):
    first = pltpu.make_async_copy(smooth_in, smooth_out, sems.at[0])
    first.start()
    copies = []
    for i in range(coarse_in.shape[0]):
        wide[i] = coarse_in[i].astype(jnp.float32)
        copy = pltpu.make_async_copy(wide.at[i], coarse_out.at[i], sems.at[1 + i])
        copy.start()
        copies.append(copy)
    first.wait()
    for copy in copies:
        copy.wait()


def widen(smooth, coarse):
    return pl.pallas_call(
        widen_kernel,
        out_shape=(
            jax.ShapeDtypeStruct(smooth.shape, jnp.float32),
            jax.ShapeDtypeStruct(coarse.shape, jnp.float32),
        ),
        in_specs=[pl.BlockSpec(memory_space=pltpu.VMEM)] * 2,
        out_specs=[pl.BlockSpec(memory_space=pltpu.HBM)] * 2,
        scratch_shapes=[pltpu.VMEM(coarse.shape, jnp.float32), pltpu.SemaphoreType.DMA((1 + coarse.shape[0],))],
        compiler_params=pltpu.CompilerParams(vmem_limit_bytes=32 << 20),
    )(smooth, coarse)


def solution(mesh):
    n_row, n_col = mesh.shape["frow"], mesh.shape["fcol"]

    def body(right_side, noise_weight, stencils, neighbours):
        rows, cols, pix = right_side.shape
        slots = stencils.shape[0]
        ext = (rows + 2 * HALO, cols + 2 * SIDE)
        tiles = ext[0] * ext[1]
        listed = jnp.transpose(neighbours, (2, 0, 1))
        smooth, coarse = pl.pallas_call(
            functools.partial(kernel, (n_row, n_col, rows, cols, pix, slots)),
            out_shape=(
                jax.ShapeDtypeStruct((rows, cols, pix), jnp.float32),
                jax.ShapeDtypeStruct((rows // 2, cols // 2 * n_col, pix), jnp.bfloat16),
            ),
            in_specs=[pl.BlockSpec(memory_space=pl.ANY)] * 4,
            out_specs=(pl.BlockSpec(memory_space=pltpu.VMEM), pl.BlockSpec(memory_space=pltpu.VMEM)),
            scratch_shapes=[
                pltpu.VMEM(ext + (pix,), jnp.float32),
                pltpu.VMEM(ext + (pix,), jnp.float32),
                pltpu.VMEM((tiles, pix), jnp.float32),
                pltpu.VMEM((HALO, 3, tiles, pix), jnp.bfloat16),
                pltpu.VMEM((slots, tiles, 128), jnp.bfloat16),
                pltpu.VMEM((pix // 128, rows * ext[1], 128), jnp.float32),
                pltpu.VMEM((slots, rows, cols), jnp.int32),
                pltpu.VMEM((slots, pix, pix), jnp.bfloat16),
                pltpu.VMEM((2 * rows * cols + cols, pix), jnp.bfloat16),
                pltpu.VMEM((2, 2 * HALO * cols + cols, pix), jnp.bfloat16),
                pltpu.VMEM((2, 2 * rows * SIDE + 2 * SIDE, pix), jnp.bfloat16),
                pltpu.VMEM((2, 2 * rows * SIDE + 2 * SIDE, pix), jnp.bfloat16),
                pltpu.VMEM((4, 2 * HALO * SIDE + 2 * SIDE, pix), jnp.bfloat16),
                pltpu.VMEM((6, SIDE, 128), jnp.float32),
                pltpu.SemaphoreType.DMA((4,)),
                pltpu.SemaphoreType.DMA((8,)),
                pltpu.SemaphoreType.DMA((8,)),
                pltpu.SemaphoreType.DMA((65,)),
                pltpu.SemaphoreType.DMA((65,)),
            ],
            compiler_params=pltpu.CompilerParams(
                collective_id=0, has_side_effects=True, vmem_limit_bytes=48 << 20,
            ),
        )(*[pltpu.with_memory_space_constraint(v, pltpu.HBM) for v in (right_side, noise_weight, stencils, listed)])
        return widen(smooth, coarse)

    placed = (P("frow", "fcol", None), P("frow", "fcol", None), P(), P("frow", "fcol", None))
    return jax.shard_map(
        body,
        mesh=mesh,
        in_specs=placed,
        out_specs=(P("frow", "fcol", None), P("frow", None, None)),
        check_vma=False,
    )
```

```python
import functools

import jax
import jax.numpy as jnp
from jax import lax
from jax.experimental import pallas as pl
from jax.experimental.pallas import tpu as pltpu
from jax.sharding import PartitionSpec as P

MESH = pl.DeviceIdType.MESH
LOWER, UPPER, DEG, SWEEPS = 1.5, 6.0, 3, 2
HALO = DEG * SWEEPS
SIDE = 8
MIDDLE = 3.75


def coefficients():
    center = 0.5 * (UPPER + LOWER)
    half_width = 0.5 * (UPPER - LOWER)
    spread = center / half_width
    steps = []
    for _ in range(SWEEPS):
        ratio = 1.0 / spread
        for step in range(DEG):
            if step < DEG - 1:
                after = 1.0 / (2.0 * spread - ratio)
                steps.append((after * ratio, 2.0 * after / half_width))
                ratio = after
            else:
                steps.append((0.0, 1.0 / center))
    return center, steps


def kernel(
    sizes, rs, nw, st, nb, sol_ref, out_ref, res, wgt, drc, dir_bf, msk, fin, own_nb, stv,
    band_out, band_in, strip_out, strip_in, corner_in, side_mask, loc_sem, h_send, h_recv, g_send, g_recv
):
    n_row, n_col, rows, cols, pix, slots = sizes
    ext_rows, ext_cols = rows + 2 * HALO, cols + 2 * SIDE
    frow, fcol = lax.axis_index("frow"), lax.axis_index("fcol")
    f32, bf16 = jnp.float32, jnp.bfloat16
    has = {"up": frow > 0, "down": frow < n_row - 1, "left": fcol > 0, "right": fcol < n_col - 1}
    beside = {"up": (frow - 1, fcol), "down": (frow + 1, fcol), "left": (frow, fcol - 1), "right": (frow, fcol + 1)}
    sides = ("up", "down", "left", "right")
    y, zh = lax.rem(fcol, 4), lax.rem(fcol // 4, 2)

    def along_x(d):
        return lax.rem(fcol + 8 * d, n_col)

    def along_y(d):
        return fcol - y + lax.rem(y + d, 4)

    partner = fcol + 4 - 8 * zh
    away = {"left": jnp.logical_and(y == 0, has["left"]), "right": jnp.logical_and(y == 3, has["right"])}
    far = jnp.logical_or(away["left"], away["right"])
    far_left = y == 0
    far_side = jnp.where(far_left, 0, 1)

    barrier = pltpu.get_barrier_semaphore()
    def hail(side):
        @pl.when(has[side])
        def _():
            pl.semaphore_signal(barrier, inc=1, device_id=beside[side], device_id_type=MESH)

    hail("left")
    hail("right")
    local = [
        pltpu.make_async_copy(nb, own_nb, loc_sem.at[0]),
        pltpu.make_async_copy(rs, res.at[pl.ds(HALO, rows), pl.ds(SIDE, cols)], loc_sem.at[1]),
        pltpu.make_async_copy(nw, wgt.at[pl.ds(HALO, rows), pl.ds(SIDE, cols)], loc_sem.at[2]),
        pltpu.make_async_copy(st, stv, loc_sem.at[3]),
    ]
    for copy in local[:3]:
        copy.start()
    hail("up")
    hail("down")
    for peer in [along_x(d) for d in (1, 2, 3)] + [along_y(d) for d in (1, 2, 3)] + [partner]:
        pl.semaphore_signal(barrier, inc=1, device_id=(frow, peer), device_id_type=MESH)

    for n, side in enumerate(("up", "down")):

        @pl.when(jnp.logical_not(has[side]))
        def _(n=n):
            band_in[n] = jnp.zeros(band_in.shape[1:], bf16)
            corner_in[2 * n] = jnp.zeros(corner_in.shape[1:], bf16)
            corner_in[2 * n + 1] = jnp.zeros(corner_in.shape[1:], bf16)

    for n, side in enumerate(("left", "right")):

        @pl.when(jnp.logical_not(has[side]))
        def _(n=n):
            strip_in[n] = jnp.zeros(strip_in.shape[1:], bf16)

    for copy in local[:3]:
        copy.wait()
    local[3].start()
    flat = jnp.where(own_nb[...] >= 0, 1.0, 0.0).astype(f32).reshape(slots * rows, cols)
    flat = jnp.concatenate([flat, jnp.zeros((128 - slots * rows, cols), f32)], axis=0)
    turned = jnp.transpose(flat)
    listed = jnp.concatenate([turned, jnp.zeros((cols, pix - 128), f32)], axis=1)
    half = rows // 2 - 1
    unit, small = 2 * cols, 2 * SIDE

    def spot(row, size, middle):
        return row * size + (middle if row >= half else 0)

    for n, c0 in ((0, 0), (1, cols - SIDE)):
        strip_out[n, pl.ds(half * small, small), :] = jnp.concatenate(
            [listed[c0 : c0 + SIDE], jnp.zeros((SIDE, pix), f32)], axis=0
        ).astype(bf16)
    for row in range(rows):
        for n, c0 in ((0, 0), (1, cols - SIDE)):
            strip_out[n, pl.ds(spot(row, small, small), small), :] = jnp.concatenate(
                [
                    res[HALO + row, pl.ds(SIDE + c0, SIDE), :],
                    wgt[HALO + row, pl.ds(SIDE + c0, SIDE), :] - MIDDLE,
                ],
                axis=0,
            ).astype(bf16)

    band_size = HALO * unit + cols
    corner_size = HALO * small + small

    def remote(src, dst, index, peer):
        return pltpu.make_async_remote_copy(
            src_ref=src, dst_ref=dst, send_sem=h_send.at[index], recv_sem=h_recv.at[index],
            device_id=peer, device_id_type=MESH,
        )

    far_band, far_strip = pl.ds((rows - HALO) * unit, band_size), pl.ds((rows - HALO) * small, corner_size)
    near_band, near_strip = pl.ds(0, band_size), pl.ds(0, corner_size)
    strips = [
        ("right", "left", lambda: remote(strip_out.at[1], strip_in.at[0], 0, beside["right"])),
        ("left", "right", lambda: remote(strip_out.at[0], strip_in.at[1], 1, beside["left"])),
    ]
    bands = [
        ("down", "up", lambda: remote(band_out.at[far_band], band_in.at[0], 2, beside["down"])),
        ("up", "down", lambda: remote(band_out.at[near_band], band_in.at[1], 3, beside["up"])),
    ]
    corners = [
        [
            ("down", "up", lambda n=n: remote(strip_in.at[n, far_strip], corner_in.at[n], 4 + n, beside["down"])),
            ("up", "down", lambda n=n: remote(strip_in.at[n, near_strip], corner_in.at[2 + n], 6 + n, beside["up"])),
        ]
        for n in range(2)
    ]

    def each(copies, act, by):
        for entry in copies:

            @pl.when(has[entry[by]])
            def _(entry=entry):
                getattr(entry[2](), act)()

    amount = 7
    for side in sides:
        amount = amount + jnp.where(has[side], 1, 0)
    pl.semaphore_wait(barrier, amount)
    each(strips, "start", 0)
    band_out[pl.ds(half * unit, cols), :] = listed.astype(bf16)
    for row in range(rows):
        r = res[HALO + row, pl.ds(SIDE, cols), :]
        w = wgt[HALO + row, pl.ds(SIDE, cols), :] - MIDDLE
        band_out[pl.ds(spot(row, unit, cols), unit), :] = jnp.concatenate([r, w], axis=0).astype(bf16)
    each(bands, "start", 0)

    def mask_rows(first, last, base, left, middle, right):
        whole = jnp.concatenate([left, middle, right], axis=0)
        for k in range(slots):
            for row in range(first, last):
                m = k * rows + row
                wide = jnp.broadcast_to(whole[:, m : m + 1], (ext_cols, 128)).astype(bf16)
                msk[k, pl.ds((base + row - first) * ext_cols, ext_cols), :] = wide

    for n, side in enumerate(("left", "right")):

        @pl.when(jnp.logical_not(away[side]))
        def _(n=n):
            each(strips[n : n + 1], "wait_recv", 1)
            each(corners[n], "start", 0)

    for m, side, c0 in ((0, "left", 0), (1, "right", SIDE + cols)):

        @pl.when(jnp.logical_not(away[side]))
        def _(m=m, c0=c0):
            for row in range(rows):
                part = strip_in[m, pl.ds(spot(row, small, small), small), :].astype(f32)
                res[HALO + row, pl.ds(c0, SIDE), :] = part[:SIDE]
                wgt[HALO + row, pl.ds(c0, SIDE), :] = part[SIDE:] + MIDDLE
            side_mask[m] = strip_in[m, pl.ds(half * small, small), :].astype(f32)[:SIDE, :128]

        @pl.when(away[side])
        def _(m=m, c0=c0):
            res[:, pl.ds(c0, SIDE), :] = jnp.zeros((ext_rows, SIDE, pix), f32)
            wgt[:, pl.ds(c0, SIDE), :] = jnp.zeros((ext_rows, SIDE, pix), f32)
            for n in range(3):
                side_mask[2 * n + m] = jnp.zeros((SIDE, 128), f32)

    mask_rows(0, rows, HALO, side_mask[0], turned, side_mask[1])
    each(bands, "wait_recv", 1)
    both = ((0, 0, rows - HALO), (1, HALO + rows, 0))
    for n, base, skip in both:
        for i in range(HALO):
            part = band_in[n, pl.ds(spot(i + skip, unit, cols) - skip * unit, unit), :].astype(f32)
            res[base + i, pl.ds(SIDE, cols), :] = part[:cols]
            wgt[base + i, pl.ds(SIDE, cols), :] = part[cols:] + MIDDLE
    for n, side in enumerate(("left", "right")):

        @pl.when(jnp.logical_not(away[side]))
        def _(n=n):
            each(corners[n], "wait_recv", 1)

    for n, base, skip in both:
        offset = half - skip
        for m, side, c0 in ((0, "left", 0), (1, "right", SIDE + cols)):

            @pl.when(jnp.logical_not(away[side]))
            def _(m=m, c0=c0, n=n, base=base, skip=skip, offset=offset):
                for i in range(HALO):
                    at = pl.ds(spot(i + skip, small, small) - skip * small, small)
                    part = corner_in[2 * n + m, at, :].astype(f32)
                    res[base + i, pl.ds(c0, SIDE), :] = part[:SIDE]
                    wgt[base + i, pl.ds(c0, SIDE), :] = part[SIDE:] + MIDDLE
                side_mask[2 + 2 * n + m] = corner_in[2 * n + m, pl.ds(offset * small, small), :].astype(f32)[:SIDE, :128]

        mask_rows(
            skip, skip + HALO, base, side_mask[2 + 2 * n],
            band_in[n, pl.ds(offset * unit, cols), :].astype(f32)[:, :128], side_mask[3 + 2 * n],
        )
    local[3].wait()

    center, steps = coefficients()

    def put(buf, t0, count, value):
        for j, shift in enumerate((1, 0, count - 1)):
            moved = value if shift == 0 else pltpu.roll(value, shift, axis=0)
            dir_bf[buf, j, pl.ds(t0, count), :] = moved.astype(jnp.bfloat16)

    res_flat = res.reshape(ext_rows * ext_cols, pix)
    wgt_flat = wgt.reshape(ext_rows * ext_cols, pix)

    def begin(i, c):
        t0 = pl.multiple_of(i * (2 * ext_cols), 2 * ext_cols)
        d = res_flat[pl.ds(t0, 2 * ext_cols), :] * (1.0 / center)
        drc[pl.ds(t0, 2 * ext_cols), :] = d
        put(0, t0, 2 * ext_cols, d)
        return c

    lax.fori_loop(0, ext_rows // 2, begin, 0)

    drc_cube = drc.reshape(ext_rows, ext_cols, pix)

    def redo():
        width = 2 * SIDE
        c0 = pl.multiple_of(jnp.where(far_left, 0, ext_cols - width), width)
        outer = pl.ds(pl.multiple_of(jnp.where(far_left, 0, ext_cols - SIDE), SIDE), SIDE)
        for row in range(rows):
            part = strip_in[far_side, pl.ds(spot(row, small, small), small), :].astype(f32)
            res[HALO + row, outer, :] = part[:SIDE]
            wgt[HALO + row, outer, :] = part[SIDE:] + MIDDLE
        def window_masks(start, stop, base, halo, inner):
            halo = halo.astype(f32)[:SIDE, :128]
            whole = jnp.where(
                far_left,
                jnp.concatenate([halo, inner[:SIDE]], axis=0),
                jnp.concatenate([inner[cols - SIDE :], halo], axis=0),
            )
            for k in range(slots):
                for row in range(start, stop):
                    m = k * rows + row
                    wide = jnp.broadcast_to(whole[:, m : m + 1], (width, 128)).astype(bf16)
                    msk[k, pl.ds(pl.multiple_of((base + row - start) * ext_cols + c0, width), width), :] = wide

        window_masks(0, rows, HALO, strip_in[far_side, pl.ds(half * small, small), :], turned)
        for n, side in enumerate(("left", "right")):

            @pl.when(away[side])
            def _(n=n):
                each(corners[n], "wait_recv", 1)

        for n, base, skip in both:
            for i in range(HALO):
                at = pl.ds(spot(i + skip, small, small) - skip * small, small)
                part = corner_in[2 * n + far_side, at, :].astype(f32)
                res[base + i, outer, :] = part[:SIDE]
                wgt[base + i, outer, :] = part[SIDE:] + MIDDLE
        for n, base, skip in both:
            offset = half - skip
            window_masks(
                skip, skip + HALO, base, corner_in[2 * n + far_side, pl.ds(offset * small, small), :],
                band_in[n, pl.ds(offset * unit, cols), :].astype(f32)[:, :128],
            )

        res_cube, dir_cube = res, dir_bf.reshape(HALO, 3, ext_rows, ext_cols, pix)
        msk_cube = msk.reshape(slots, ext_rows, ext_cols, 128)
        span = pl.ds(c0, width)

        def edges(count):
            inside = lax.broadcasted_iota(jnp.int32, (count, width, pix), 1).reshape(count * width, pix)
            return inside, jnp.where(far_left, inside, width - 1 - inside)

        def put_window(level, first, count, value):
            at = pl.ds(first, count)
            inside, edge = edges(count)

            def held(j):
                return dir_cube[level, j, at, span, :].reshape(count * width, pix).astype(f32)

            value = jnp.where(edge < SIDE + level, value, held(1))
            back = jnp.where(inside == 0, held(0), pltpu.roll(value, 1, axis=0))
            ahead = jnp.where(inside == width - 1, held(2), pltpu.roll(value, count * width - 1, axis=0))
            for j, moved in enumerate((back, value, ahead)):
                dir_cube[level, j, at, span, :] = moved.astype(bf16).reshape(count, width, pix)

        def get(cube, first, count):
            return cube[pl.ds(first, count), span, :].reshape(count * width, pix)

        start = get(res_cube, 0, ext_rows) * (1.0 / center)
        _, edge = edges(ext_rows)
        start = jnp.where(edge < SIDE, start, get(drc_cube, 0, ext_rows))
        drc_cube[:, span, :] = start.reshape(ext_rows, width, pix)
        put_window(0, 0, ext_rows, start)
        inner_span = pl.ds(pl.multiple_of(jnp.where(far_left, SIDE, ext_cols - width), SIDE), SIDE)
        sol_span = pl.ds(pl.multiple_of(jnp.where(far_left, 0, cols - SIDE), SIDE), SIDE)
        within = lax.broadcasted_iota(jnp.int32, (rows, SIDE, pix), 1)
        within = jnp.where(far_left, within, SIDE - 1 - within)
        for op in range(AWAIT + 1):
            low = op + 1
            count = ext_rows - 2 * low
            if op > 0:
                more = drc_cube[pl.ds(HALO, rows), inner_span, :]
                sol_ref[:, sol_span, :] = sol_ref[:, sol_span, :] + jnp.where(within < op, more, 0.0)
            parts = []
            for k in range(slots):
                part = dir_cube[op, k % 3, pl.ds(low + k // 3 - 1, count), span, :].reshape(count * width, pix)
                keep = msk_cube[k, pl.ds(low, count), span, :].reshape(count * width, 128)
                parts.append(part * jnp.concatenate([keep, keep], axis=1))
            coupled = jnp.dot(
                jnp.concatenate(parts, axis=1), stv[...].reshape(slots * pix, pix), preferred_element_type=f32
            )
            d, old_r = get(drc_cube, low, count), get(res_cube, low, count)
            r = old_r - (get(wgt, low, count) * d + coupled)
            _, edge = edges(count)
            exact = edge < SIDE + low
            old, new = steps[op]
            after = new * r if old == 0.0 else old * d + new * r
            res_cube[pl.ds(low, count), span, :] = jnp.where(exact, r, old_r).reshape(count, width, pix)
            drc_cube[pl.ds(low, count), span, :] = jnp.where(exact, after, d).reshape(count, width, pix)
            put_window(low, low, count, after)

    for op in range(HALO):
        now, later = op, op + 1
        low = op + 1
        count = ext_rows - 2 * low
        chunk = CHUNK[op]
        size = chunk * ext_cols
        low_col = jnp.where(away["left"], SIDE + op, 0) if op <= AWAIT else 0
        high_col = jnp.where(away["right"], SIDE + cols - op, ext_cols) if op <= AWAIT else ext_cols
        own = drc_cube[pl.ds(HALO, rows), pl.ds(SIDE, cols), :]
        at_col = lax.broadcasted_iota(jnp.int32, (rows, cols, pix), 1) + SIDE
        own = jnp.where(jnp.logical_and(at_col >= low_col, at_col < high_col), own, 0.0)
        sol_ref[...] = own if op == 0 else sol_ref[...] + own

        def apply(i, c, now=now, later=later, low=low, size=size, op=op, low_col=low_col, high_col=high_col):
            t0 = pl.multiple_of(low * ext_cols + i * size, ext_cols)
            parts = []
            for k in range(slots):
                src = t0 + (k // 3 - 1) * ext_cols
                part = dir_bf[now, k % 3, pl.ds(pl.multiple_of(src, ext_cols), size), :]
                keep = msk[k, pl.ds(t0, size), :]
                parts.append(part * jnp.concatenate([keep, keep], axis=1))
            coupled = jnp.dot(
                jnp.concatenate(parts, axis=1), stv[...].reshape(slots * pix, pix), preferred_element_type=jnp.float32
            )
            d = drc[pl.ds(t0, size), :]
            old_r = res_flat[pl.ds(t0, size), :]
            r = old_r - (wgt_flat[pl.ds(t0, size), :] * d + coupled)
            col = lax.broadcasted_iota(jnp.int32, (size // ext_cols, ext_cols, pix), 1).reshape(size, pix)
            exact = jnp.logical_and(col > low_col, col < high_col - 1)
            if op == HALO - 1:
                for h in range(pix // 128):
                    fin[h] = r[:, h * 128 : (h + 1) * 128]
            else:
                res_flat[pl.ds(t0, size), :] = jnp.where(exact, r, old_r)
                old, new = steps[op]
                after = new * r if old == 0.0 else old * d + new * r
                drc[pl.ds(t0, size), :] = jnp.where(exact, after, d)
                put(later, t0, size, after)
            return c

        trips = count // chunk
        if trips == 1:
            apply(0, 0)
        else:
            lax.fori_loop(0, trips, apply, 0)
        if op == ASK:
            for n, side in enumerate(("left", "right")):

                @pl.when(away[side])
                def _(n=n):
                    each(strips[n : n + 1], "wait_recv", 1)
                    each(corners[n], "start", 0)

        if op == AWAIT:
            pl.when(far)(redo)

    pixel = lax.broadcasted_iota(jnp.int32, (pix, 128), 0)
    lane = lax.broadcasted_iota(jnp.int32, (pix, 128), 1)
    fold = jnp.where(pixel // 4 == lane % 64, 1.0, 0.0).astype(jnp.bfloat16)
    pieces = []
    for a in range(2):
        for b in range(2):
            for R in range(rows // 2):
                begin_at = (2 * R + a) * ext_cols + SIDE + b
                pieces.append(
                    jnp.concatenate(
                        [fin[h, pl.ds(begin_at, cols // 2, stride=2), :] for h in range(pix // 128)], axis=1
                    )
                )
    stack = jnp.concatenate(pieces, axis=0)
    high = stack.astype(jnp.bfloat16)
    low_part = (stack - high.astype(jnp.float32)).astype(jnp.bfloat16)
    summed = jnp.dot(high, fold, preferred_element_type=jnp.float32) + jnp.dot(
        low_part, fold, preferred_element_type=jnp.float32
    )
    quarter = (rows // 2) * (cols // 2)
    quads = [summed[q * quarter : (q + 1) * quarter] for q in range(4)]
    left = lax.broadcasted_iota(jnp.int32, (quarter, 128), 1) < 64
    coarse = jnp.concatenate([jnp.where(left, quads[0], quads[1]), jnp.where(left, quads[2], quads[3])], axis=1).astype(jnp.bfloat16)
    quarter_cols = cols // 2
    group = rows // 4

    def block(j, half=None):
        span = pl.ds(pl.multiple_of(j * quarter_cols, quarter_cols), quarter_cols)
        if half is None:
            return out_ref.at[:, span, :]
        return out_ref.at[pl.ds(half * group, group), span, :]

    out_ref[:, pl.ds(pl.multiple_of(fcol * quarter_cols, quarter_cols), quarter_cols), :] = coarse.reshape(
        rows // 2, quarter_cols, pix
    )

    def move(ref, index, peer):
        return pltpu.make_async_remote_copy(
            src_ref=ref, dst_ref=ref, send_sem=g_send.at[index], recv_sem=g_recv.at[index],
            device_id=(frow, peer), device_id_type=MESH,
        )

    routes = ((along_x, along_y), (along_y, along_x))

    def source(way, d, which):
        return way((4 - d) % 4) + which * (4 - 8 * zh)

    def index_of(which, half, d1, d2):
        return 1 + ((which * 2 + half) * 4 + d1) * 4 + d2

    sent = [move(block(fcol), 0, partner)]
    sent[0].start()
    near = (1, 3, 2)

    def begin_move(ref, index, peer):
        copy = move(ref, index, peer)
        copy.start()
        sent.append(copy)

    def spread(which):
        for stage in range(2):
            for half in range(2):
                ref = block(fcol + which * (4 - 8 * zh), half)
                for d in near:
                    key = index_of(which, half, d, 0) if stage == 0 else index_of(which, half, 0, d)
                    begin_move(ref, key, routes[half][stage](d))

    def pass_on(which, half):
        for d1 in near:
            ref = block(source(routes[half][0], d1, which), half)
            move(ref, index_of(which, half, d1, 0), fcol).wait_recv()
            for d2 in near:
                begin_move(ref, index_of(which, half, d1, d2), routes[half][1](d2))

    spread(0)
    pass_on(0, 0)
    move(block(partner), 0, partner).wait_recv()
    spread(1)
    pass_on(0, 1)
    pass_on(1, 0)
    pass_on(1, 1)
    for which in range(2):
        for half in range(2):
            for d1 in (0,) + near:
                for d2 in near:
                    move(block(fcol, half), index_of(which, half, d1, d2), fcol).wait_recv()
    for copy in sent:
        copy.wait_send()
    each(strips, "wait_send", 0)
    each(bands, "wait_send", 0)
    for n in range(2):
        each(corners[n], "wait_send", 0)


ASK, AWAIT = 0, 2
CHUNK = (9, 8, 7, 6, 5, 8)


def widen_kernel(smooth_in, coarse_in, smooth_out, coarse_out, wide, sems):
    first = pltpu.make_async_copy(smooth_in, smooth_out, sems.at[0])
    first.start()
    copies = []
    for i in range(coarse_in.shape[0]):
        wide[i] = coarse_in[i].astype(jnp.float32)
        copy = pltpu.make_async_copy(wide.at[i], coarse_out.at[i], sems.at[1 + i])
        copy.start()
        copies.append(copy)
    first.wait()
    for copy in copies:
        copy.wait()


def widen(smooth, coarse):
    return pl.pallas_call(
        widen_kernel,
        out_shape=(
            jax.ShapeDtypeStruct(smooth.shape, jnp.float32),
            jax.ShapeDtypeStruct(coarse.shape, jnp.float32),
        ),
        in_specs=[pl.BlockSpec(memory_space=pltpu.VMEM)] * 2,
        out_specs=[pl.BlockSpec(memory_space=pltpu.HBM)] * 2,
        scratch_shapes=[pltpu.VMEM(coarse.shape, jnp.float32), pltpu.SemaphoreType.DMA((1 + coarse.shape[0],))],
        compiler_params=pltpu.CompilerParams(vmem_limit_bytes=32 << 20),
    )(smooth, coarse)


def solution(mesh):
    n_row, n_col = mesh.shape["frow"], mesh.shape["fcol"]

    def body(right_side, noise_weight, stencils, neighbours):
        rows, cols, pix = right_side.shape
        slots = stencils.shape[0]
        ext = (rows + 2 * HALO, cols + 2 * SIDE)
        tiles = ext[0] * ext[1]
        listed = jnp.transpose(neighbours, (2, 0, 1))
        smooth, coarse = pl.pallas_call(
            functools.partial(kernel, (n_row, n_col, rows, cols, pix, slots)),
            out_shape=(
                jax.ShapeDtypeStruct((rows, cols, pix), jnp.float32),
                jax.ShapeDtypeStruct((rows // 2, cols // 2 * n_col, pix), jnp.bfloat16),
            ),
            in_specs=[pl.BlockSpec(memory_space=pl.ANY)] * 4,
            out_specs=(pl.BlockSpec(memory_space=pltpu.VMEM), pl.BlockSpec(memory_space=pltpu.VMEM)),
            scratch_shapes=[
                pltpu.VMEM(ext + (pix,), jnp.float32),
                pltpu.VMEM(ext + (pix,), jnp.float32),
                pltpu.VMEM((tiles, pix), jnp.float32),
                pltpu.VMEM((HALO, 3, tiles, pix), jnp.bfloat16),
                pltpu.VMEM((slots, tiles, 128), jnp.bfloat16),
                pltpu.VMEM((pix // 128, rows * ext[1], 128), jnp.float32),
                pltpu.VMEM((slots, rows, cols), jnp.int32),
                pltpu.VMEM((slots, pix, pix), jnp.bfloat16),
                pltpu.VMEM((2 * rows * cols + cols, pix), jnp.bfloat16),
                pltpu.VMEM((2, 2 * HALO * cols + cols, pix), jnp.bfloat16),
                pltpu.VMEM((2, 2 * rows * SIDE + 2 * SIDE, pix), jnp.bfloat16),
                pltpu.VMEM((2, 2 * rows * SIDE + 2 * SIDE, pix), jnp.bfloat16),
                pltpu.VMEM((4, 2 * HALO * SIDE + 2 * SIDE, pix), jnp.bfloat16),
                pltpu.VMEM((6, SIDE, 128), jnp.float32),
                pltpu.SemaphoreType.DMA((4,)),
                pltpu.SemaphoreType.DMA((8,)),
                pltpu.SemaphoreType.DMA((8,)),
                pltpu.SemaphoreType.DMA((65,)),
                pltpu.SemaphoreType.DMA((65,)),
            ],
            compiler_params=pltpu.CompilerParams(
                collective_id=0, has_side_effects=True, vmem_limit_bytes=48 << 20,
            ),
        )(*[pltpu.with_memory_space_constraint(v, pltpu.HBM) for v in (right_side, noise_weight, stencils, listed)])
        return widen(smooth, coarse)

    placed = (P("frow", "fcol", None), P("frow", "fcol", None), P(), P("frow", "fcol", None))
    return jax.shard_map(
        body,
        mesh=mesh,
        in_specs=placed,
        out_specs=(P("frow", "fcol", None), P("frow", None, None)),
        check_vma=False,
    )
```

```python
import functools

import jax
import jax.numpy as jnp
from jax import lax
from jax.experimental import pallas as pl
from jax.experimental.pallas import tpu as pltpu
from jax.sharding import PartitionSpec as P

MESH = pl.DeviceIdType.MESH
LOWER, UPPER, DEG, SWEEPS = 1.5, 6.0, 3, 2
HALO = DEG * SWEEPS
SIDE = 8
MIDDLE = 3.75


def coefficients():
    center = 0.5 * (UPPER + LOWER)
    half_width = 0.5 * (UPPER - LOWER)
    spread = center / half_width
    steps = []
    for _ in range(SWEEPS):
        ratio = 1.0 / spread
        for step in range(DEG):
            if step < DEG - 1:
                after = 1.0 / (2.0 * spread - ratio)
                steps.append((after * ratio, 2.0 * after / half_width))
                ratio = after
            else:
                steps.append((0.0, 1.0 / center))
    return center, steps


def kernel(
    sizes, rs, nw, st, nb, sol_ref, out_ref, res, wgt, drc, dir_bf, msk, fin, own_nb, stv,
    band_out, band_in, strip_out, strip_in, corner_in, side_mask, loc_sem, h_send, h_recv, g_send, g_recv
):
    n_row, n_col, rows, cols, pix, slots = sizes
    ext_rows, ext_cols = rows + 2 * HALO, cols + 2 * SIDE
    frow, fcol = lax.axis_index("frow"), lax.axis_index("fcol")
    f32, bf16 = jnp.float32, jnp.bfloat16
    has = {"up": frow > 0, "down": frow < n_row - 1, "left": fcol > 0, "right": fcol < n_col - 1}
    beside = {"up": (frow - 1, fcol), "down": (frow + 1, fcol), "left": (frow, fcol - 1), "right": (frow, fcol + 1)}
    sides = ("up", "down", "left", "right")
    y, zh = lax.rem(fcol, 4), lax.rem(fcol // 4, 2)

    def along_x(d):
        return lax.rem(fcol + 8 * d, n_col)

    def along_y(d):
        return fcol - y + lax.rem(y + d, 4)

    partner = fcol + 4 - 8 * zh
    away = {"left": jnp.logical_and(y == 0, has["left"]), "right": jnp.logical_and(y == 3, has["right"])}
    far = jnp.logical_or(away["left"], away["right"])
    far_left = y == 0
    far_side = jnp.where(far_left, 0, 1)

    barrier = pltpu.get_barrier_semaphore()
    def hail(side):
        @pl.when(has[side])
        def _():
            pl.semaphore_signal(barrier, inc=1, device_id=beside[side], device_id_type=MESH)

    hail("left")
    hail("right")
    local = [
        pltpu.make_async_copy(nb, own_nb, loc_sem.at[0]),
        pltpu.make_async_copy(rs, res.at[pl.ds(HALO, rows), pl.ds(SIDE, cols)], loc_sem.at[1]),
        pltpu.make_async_copy(nw, wgt.at[pl.ds(HALO, rows), pl.ds(SIDE, cols)], loc_sem.at[2]),
        pltpu.make_async_copy(st, stv, loc_sem.at[3]),
    ]
    for copy in local[:3]:
        copy.start()
    hail("up")
    hail("down")
    for peer in [along_x(d) for d in (1, 2, 3)] + [along_y(d) for d in (1, 2, 3)] + [partner]:
        pl.semaphore_signal(barrier, inc=1, device_id=(frow, peer), device_id_type=MESH)

    for n, side in enumerate(("up", "down")):

        @pl.when(jnp.logical_not(has[side]))
        def _(n=n):
            band_in[n] = jnp.zeros(band_in.shape[1:], bf16)
            corner_in[2 * n] = jnp.zeros(corner_in.shape[1:], bf16)
            corner_in[2 * n + 1] = jnp.zeros(corner_in.shape[1:], bf16)

    for n, side in enumerate(("left", "right")):

        @pl.when(jnp.logical_not(has[side]))
        def _(n=n):
            strip_in[n] = jnp.zeros(strip_in.shape[1:], bf16)

    for copy in local[:3]:
        copy.wait()
    local[3].start()
    flat = jnp.where(own_nb[...] >= 0, 1.0, 0.0).astype(f32).reshape(slots * rows, cols)
    flat = jnp.concatenate([flat, jnp.zeros((128 - slots * rows, cols), f32)], axis=0)
    turned = jnp.transpose(flat)
    listed = jnp.concatenate([turned, jnp.zeros((cols, pix - 128), f32)], axis=1)
    half = rows // 2 - 1
    unit, small = 2 * cols, 2 * SIDE

    def spot(row, size, middle):
        return row * size + (middle if row >= half else 0)

    for n, c0 in ((0, 0), (1, cols - SIDE)):
        strip_out[n, pl.ds(half * small, small), :] = jnp.concatenate(
            [listed[c0 : c0 + SIDE], jnp.zeros((SIDE, pix), f32)], axis=0
        ).astype(bf16)
    for row in range(rows):
        for n, c0 in ((0, 0), (1, cols - SIDE)):
            strip_out[n, pl.ds(spot(row, small, small), small), :] = jnp.concatenate(
                [
                    res[HALO + row, pl.ds(SIDE + c0, SIDE), :],
                    wgt[HALO + row, pl.ds(SIDE + c0, SIDE), :] - MIDDLE,
                ],
                axis=0,
            ).astype(bf16)

    band_size = HALO * unit + cols
    corner_size = HALO * small + small

    def remote(src, dst, index, peer):
        return pltpu.make_async_remote_copy(
            src_ref=src, dst_ref=dst, send_sem=h_send.at[index], recv_sem=h_recv.at[index],
            device_id=peer, device_id_type=MESH,
        )

    far_band, far_strip = pl.ds((rows - HALO) * unit, band_size), pl.ds((rows - HALO) * small, corner_size)
    near_band, near_strip = pl.ds(0, band_size), pl.ds(0, corner_size)
    strips = [
        ("right", "left", lambda: remote(strip_out.at[1], strip_in.at[0], 0, beside["right"])),
        ("left", "right", lambda: remote(strip_out.at[0], strip_in.at[1], 1, beside["left"])),
    ]
    bands = [
        ("down", "up", lambda: remote(band_out.at[far_band], band_in.at[0], 2, beside["down"])),
        ("up", "down", lambda: remote(band_out.at[near_band], band_in.at[1], 3, beside["up"])),
    ]
    corners = [
        [
            ("down", "up", lambda n=n: remote(strip_in.at[n, far_strip], corner_in.at[n], 4 + n, beside["down"])),
            ("up", "down", lambda n=n: remote(strip_in.at[n, near_strip], corner_in.at[2 + n], 6 + n, beside["up"])),
        ]
        for n in range(2)
    ]

    def each(copies, act, by):
        for entry in copies:

            @pl.when(has[entry[by]])
            def _(entry=entry):
                getattr(entry[2](), act)()

    amount = 7
    for side in sides:
        amount = amount + jnp.where(has[side], 1, 0)
    pl.semaphore_wait(barrier, amount)
    each(strips, "start", 0)
    band_out[pl.ds(half * unit, cols), :] = listed.astype(bf16)
    for row in range(rows):
        r = res[HALO + row, pl.ds(SIDE, cols), :]
        w = wgt[HALO + row, pl.ds(SIDE, cols), :] - MIDDLE
        band_out[pl.ds(spot(row, unit, cols), unit), :] = jnp.concatenate([r, w], axis=0).astype(bf16)
    each(bands, "start", 0)

    def mask_rows(first, last, base, left, middle, right):
        whole = jnp.concatenate([left, middle, right], axis=0)
        for k in range(slots):
            for row in range(first, last):
                m = k * rows + row
                wide = jnp.broadcast_to(whole[:, m : m + 1], (ext_cols, 128)).astype(bf16)
                msk[k, pl.ds((base + row - first) * ext_cols, ext_cols), :] = wide

    for n, side in enumerate(("left", "right")):

        @pl.when(jnp.logical_not(away[side]))
        def _(n=n):
            each(strips[n : n + 1], "wait_recv", 1)
            each(corners[n], "start", 0)

    for m, side, c0 in ((0, "left", 0), (1, "right", SIDE + cols)):

        @pl.when(jnp.logical_not(away[side]))
        def _(m=m, c0=c0):
            for row in range(rows):
                part = strip_in[m, pl.ds(spot(row, small, small), small), :].astype(f32)
                res[HALO + row, pl.ds(c0, SIDE), :] = part[:SIDE]
                wgt[HALO + row, pl.ds(c0, SIDE), :] = part[SIDE:] + MIDDLE
            side_mask[m] = strip_in[m, pl.ds(half * small, small), :].astype(f32)[:SIDE, :128]

        @pl.when(away[side])
        def _(m=m, c0=c0):
            res[:, pl.ds(c0, SIDE), :] = jnp.zeros((ext_rows, SIDE, pix), f32)
            wgt[:, pl.ds(c0, SIDE), :] = jnp.zeros((ext_rows, SIDE, pix), f32)
            for n in range(3):
                side_mask[2 * n + m] = jnp.zeros((SIDE, 128), f32)

    mask_rows(0, rows, HALO, side_mask[0], turned, side_mask[1])
    each(bands, "wait_recv", 1)
    both = ((0, 0, rows - HALO), (1, HALO + rows, 0))
    for n, base, skip in both:
        for i in range(HALO):
            part = band_in[n, pl.ds(spot(i + skip, unit, cols) - skip * unit, unit), :].astype(f32)
            res[base + i, pl.ds(SIDE, cols), :] = part[:cols]
            wgt[base + i, pl.ds(SIDE, cols), :] = part[cols:] + MIDDLE
    for n, side in enumerate(("left", "right")):

        @pl.when(jnp.logical_not(away[side]))
        def _(n=n):
            each(corners[n], "wait_recv", 1)

    for n, base, skip in both:
        offset = half - skip
        for m, side, c0 in ((0, "left", 0), (1, "right", SIDE + cols)):

            @pl.when(jnp.logical_not(away[side]))
            def _(m=m, c0=c0, n=n, base=base, skip=skip, offset=offset):
                for i in range(HALO):
                    at = pl.ds(spot(i + skip, small, small) - skip * small, small)
                    part = corner_in[2 * n + m, at, :].astype(f32)
                    res[base + i, pl.ds(c0, SIDE), :] = part[:SIDE]
                    wgt[base + i, pl.ds(c0, SIDE), :] = part[SIDE:] + MIDDLE
                side_mask[2 + 2 * n + m] = corner_in[2 * n + m, pl.ds(offset * small, small), :].astype(f32)[:SIDE, :128]

        mask_rows(
            skip, skip + HALO, base, side_mask[2 + 2 * n],
            band_in[n, pl.ds(offset * unit, cols), :].astype(f32)[:, :128], side_mask[3 + 2 * n],
        )
    local[3].wait()

    center, steps = coefficients()

    def put(buf, t0, count, value):
        for j, shift in enumerate((1, 0, count - 1)):
            moved = value if shift == 0 else pltpu.roll(value, shift, axis=0)
            dir_bf[buf, j, pl.ds(t0, count), :] = moved.astype(jnp.bfloat16)

    res_flat = res.reshape(ext_rows * ext_cols, pix)
    wgt_flat = wgt.reshape(ext_rows * ext_cols, pix)

    def begin(i, c):
        t0 = pl.multiple_of(i * (2 * ext_cols), 2 * ext_cols)
        d = res_flat[pl.ds(t0, 2 * ext_cols), :] * (1.0 / center)
        drc[pl.ds(t0, 2 * ext_cols), :] = d
        put(0, t0, 2 * ext_cols, d)
        return c

    lax.fori_loop(0, ext_rows // 2, begin, 0)

    drc_cube = drc.reshape(ext_rows, ext_cols, pix)

    def redo():
        width = 2 * SIDE
        c0 = pl.multiple_of(jnp.where(far_left, 0, ext_cols - width), width)
        outer = pl.ds(pl.multiple_of(jnp.where(far_left, 0, ext_cols - SIDE), SIDE), SIDE)
        for row in range(rows):
            part = strip_in[far_side, pl.ds(spot(row, small, small), small), :].astype(f32)
            res[HALO + row, outer, :] = part[:SIDE]
            wgt[HALO + row, outer, :] = part[SIDE:] + MIDDLE
        def window_masks(start, stop, base, halo, inner):
            halo = halo.astype(f32)[:SIDE, :128]
            whole = jnp.where(
                far_left,
                jnp.concatenate([halo, inner[:SIDE]], axis=0),
                jnp.concatenate([inner[cols - SIDE :], halo], axis=0),
            )
            for k in range(slots):
                for row in range(start, stop):
                    m = k * rows + row
                    wide = jnp.broadcast_to(whole[:, m : m + 1], (width, 128)).astype(bf16)
                    msk[k, pl.ds(pl.multiple_of((base + row - start) * ext_cols + c0, width), width), :] = wide

        window_masks(0, rows, HALO, strip_in[far_side, pl.ds(half * small, small), :], turned)
        for n, side in enumerate(("left", "right")):

            @pl.when(away[side])
            def _(n=n):
                each(corners[n], "wait_recv", 1)

        for n, base, skip in both:
            for i in range(HALO):
                at = pl.ds(spot(i + skip, small, small) - skip * small, small)
                part = corner_in[2 * n + far_side, at, :].astype(f32)
                res[base + i, outer, :] = part[:SIDE]
                wgt[base + i, outer, :] = part[SIDE:] + MIDDLE
        for n, base, skip in both:
            offset = half - skip
            window_masks(
                skip, skip + HALO, base, corner_in[2 * n + far_side, pl.ds(offset * small, small), :],
                band_in[n, pl.ds(offset * unit, cols), :].astype(f32)[:, :128],
            )

        res_cube, dir_cube = res, dir_bf.reshape(HALO, 3, ext_rows, ext_cols, pix)
        msk_cube = msk.reshape(slots, ext_rows, ext_cols, 128)
        span = pl.ds(c0, width)

        def edges(count):
            inside = lax.broadcasted_iota(jnp.int32, (count, width, pix), 1).reshape(count * width, pix)
            return inside, jnp.where(far_left, inside, width - 1 - inside)

        def put_window(level, first, count, value):
            at = pl.ds(first, count)
            inside, edge = edges(count)

            def held(j):
                return dir_cube[level, j, at, span, :].reshape(count * width, pix).astype(f32)

            value = jnp.where(edge < SIDE + level, value, held(1))
            back = jnp.where(inside == 0, held(0), pltpu.roll(value, 1, axis=0))
            ahead = jnp.where(inside == width - 1, held(2), pltpu.roll(value, count * width - 1, axis=0))
            for j, moved in enumerate((back, value, ahead)):
                dir_cube[level, j, at, span, :] = moved.astype(bf16).reshape(count, width, pix)

        def get(cube, first, count):
            return cube[pl.ds(first, count), span, :].reshape(count * width, pix)

        start = get(res_cube, 0, ext_rows) * (1.0 / center)
        _, edge = edges(ext_rows)
        start = jnp.where(edge < SIDE, start, get(drc_cube, 0, ext_rows))
        drc_cube[:, span, :] = start.reshape(ext_rows, width, pix)
        put_window(0, 0, ext_rows, start)
        inner_span = pl.ds(pl.multiple_of(jnp.where(far_left, SIDE, ext_cols - width), SIDE), SIDE)
        sol_span = pl.ds(pl.multiple_of(jnp.where(far_left, 0, cols - SIDE), SIDE), SIDE)
        within = lax.broadcasted_iota(jnp.int32, (rows, SIDE, pix), 1)
        within = jnp.where(far_left, within, SIDE - 1 - within)
        for op in range(AWAIT + 1):
            low = op + 1
            count = ext_rows - 2 * low
            if op > 0:
                more = drc_cube[pl.ds(HALO, rows), inner_span, :]
                sol_ref[:, sol_span, :] = sol_ref[:, sol_span, :] + jnp.where(within < op, more, 0.0)
            parts = []
            for k in range(slots):
                part = dir_cube[op, k % 3, pl.ds(low + k // 3 - 1, count), span, :].reshape(count * width, pix)
                keep = msk_cube[k, pl.ds(low, count), span, :].reshape(count * width, 128)
                parts.append(part * jnp.concatenate([keep, keep], axis=1))
            coupled = jnp.dot(
                jnp.concatenate(parts, axis=1), stv[...].reshape(slots * pix, pix), preferred_element_type=f32
            )
            d, old_r = get(drc_cube, low, count), get(res_cube, low, count)
            r = old_r - (get(wgt, low, count) * d + coupled)
            _, edge = edges(count)
            exact = edge < SIDE + low
            old, new = steps[op]
            after = new * r if old == 0.0 else old * d + new * r
            res_cube[pl.ds(low, count), span, :] = jnp.where(exact, r, old_r).reshape(count, width, pix)
            drc_cube[pl.ds(low, count), span, :] = jnp.where(exact, after, d).reshape(count, width, pix)
            put_window(low, low, count, after)

    for op in range(HALO):
        now, later = op, op + 1
        low = op + 1
        count = ext_rows - 2 * low
        chunk = CHUNK[op]
        size = chunk * ext_cols
        low_col = jnp.where(away["left"], SIDE + op, 0) if op <= AWAIT else 0
        high_col = jnp.where(away["right"], SIDE + cols - op, ext_cols) if op <= AWAIT else ext_cols
        own = drc_cube[pl.ds(HALO, rows), pl.ds(SIDE, cols), :]
        at_col = lax.broadcasted_iota(jnp.int32, (rows, cols, pix), 1) + SIDE
        own = jnp.where(jnp.logical_and(at_col >= low_col, at_col < high_col), own, 0.0)
        sol_ref[...] = own if op == 0 else sol_ref[...] + own

        def apply(i, c, now=now, later=later, low=low, size=size, op=op, low_col=low_col, high_col=high_col):
            t0 = pl.multiple_of(low * ext_cols + i * size, ext_cols)
            parts = []
            for k in range(slots):
                src = t0 + (k // 3 - 1) * ext_cols
                part = dir_bf[now, k % 3, pl.ds(pl.multiple_of(src, ext_cols), size), :]
                keep = msk[k, pl.ds(t0, size), :]
                parts.append(part * jnp.concatenate([keep, keep], axis=1))
            coupled = jnp.dot(
                jnp.concatenate(parts, axis=1), stv[...].reshape(slots * pix, pix), preferred_element_type=jnp.float32
            )
            d = drc[pl.ds(t0, size), :]
            old_r = res_flat[pl.ds(t0, size), :]
            r = old_r - (wgt_flat[pl.ds(t0, size), :] * d + coupled)
            col = lax.broadcasted_iota(jnp.int32, (size // ext_cols, ext_cols, pix), 1).reshape(size, pix)
            exact = jnp.logical_and(col > low_col, col < high_col - 1)
            if op == HALO - 1:
                for h in range(pix // 128):
                    fin[h] = r[:, h * 128 : (h + 1) * 128]
            else:
                res_flat[pl.ds(t0, size), :] = jnp.where(exact, r, old_r)
                old, new = steps[op]
                after = new * r if old == 0.0 else old * d + new * r
                drc[pl.ds(t0, size), :] = jnp.where(exact, after, d)
                put(later, t0, size, after)
            return c

        trips = count // chunk
        if trips == 1:
            apply(0, 0)
        else:
            lax.fori_loop(0, trips, apply, 0)
        if op == ASK:
            for n, side in enumerate(("left", "right")):

                @pl.when(away[side])
                def _(n=n):
                    each(strips[n : n + 1], "wait_recv", 1)
                    each(corners[n], "start", 0)

        if op == AWAIT:
            pl.when(far)(redo)

    pixel = lax.broadcasted_iota(jnp.int32, (pix, 128), 0)
    lane = lax.broadcasted_iota(jnp.int32, (pix, 128), 1)
    fold = jnp.where(pixel // 4 == lane % 64, 1.0, 0.0).astype(jnp.bfloat16)
    pieces = []
    for a in range(2):
        for b in range(2):
            for R in range(rows // 2):
                begin_at = (2 * R + a) * ext_cols + SIDE + b
                pieces.append(
                    jnp.concatenate(
                        [fin[h, pl.ds(begin_at, cols // 2, stride=2), :] for h in range(pix // 128)], axis=1
                    )
                )
    stack = jnp.concatenate(pieces, axis=0)
    high = stack.astype(jnp.bfloat16)
    low_part = (stack - high.astype(jnp.float32)).astype(jnp.bfloat16)
    summed = jnp.dot(high, fold, preferred_element_type=jnp.float32) + jnp.dot(
        low_part, fold, preferred_element_type=jnp.float32
    )
    quarter = (rows // 2) * (cols // 2)
    quads = [summed[q * quarter : (q + 1) * quarter] for q in range(4)]
    left = lax.broadcasted_iota(jnp.int32, (quarter, 128), 1) < 64
    coarse = jnp.concatenate([jnp.where(left, quads[0], quads[1]), jnp.where(left, quads[2], quads[3])], axis=1).astype(jnp.bfloat16)
    quarter_cols = cols // 2
    group = rows // 4

    def block(j, half=None):
        span = pl.ds(pl.multiple_of(j * quarter_cols, quarter_cols), quarter_cols)
        if half is None:
            return out_ref.at[:, span, :]
        return out_ref.at[pl.ds(half * group, group), span, :]

    out_ref[:, pl.ds(pl.multiple_of(fcol * quarter_cols, quarter_cols), quarter_cols), :] = coarse.reshape(
        rows // 2, quarter_cols, pix
    )

    def move(ref, index, peer):
        return pltpu.make_async_remote_copy(
            src_ref=ref, dst_ref=ref, send_sem=g_send.at[index], recv_sem=g_recv.at[index],
            device_id=(frow, peer), device_id_type=MESH,
        )

    routes = ((along_x, along_y), (along_y, along_x))

    def source(way, d, which):
        return way((4 - d) % 4) + which * (4 - 8 * zh)

    def index_of(which, half, d1, d2):
        return 1 + ((which * 2 + half) * 4 + d1) * 4 + d2

    sent = [move(block(fcol), 0, partner)]
    sent[0].start()
    near = (2, 1, 3)

    def begin_move(ref, index, peer):
        copy = move(ref, index, peer)
        copy.start()
        sent.append(copy)

    def spread(which):
        for stage in range(2):
            for half in range(2):
                ref = block(fcol + which * (4 - 8 * zh), half)
                for d in near:
                    key = index_of(which, half, d, 0) if stage == 0 else index_of(which, half, 0, d)
                    begin_move(ref, key, routes[half][stage](d))

    def pass_on(which, half):
        for d1 in near:
            ref = block(source(routes[half][0], d1, which), half)
            move(ref, index_of(which, half, d1, 0), fcol).wait_recv()
            for d2 in near:
                begin_move(ref, index_of(which, half, d1, d2), routes[half][1](d2))

    spread(0)
    pass_on(0, 0)
    move(block(partner), 0, partner).wait_recv()
    spread(1)
    pass_on(0, 1)
    pass_on(1, 0)
    pass_on(1, 1)
    for which in range(2):
        for half in range(2):
            for d1 in (0,) + near:
                for d2 in near:
                    move(block(fcol, half), index_of(which, half, d1, d2), fcol).wait_recv()
    for copy in sent:
        copy.wait_send()
    each(strips, "wait_send", 0)
    each(bands, "wait_send", 0)
    for n in range(2):
        each(corners[n], "wait_send", 0)


ASK, AWAIT = 0, 2
CHUNK = (9, 8, 7, 6, 5, 8)


def widen_kernel(smooth_in, coarse_in, smooth_out, coarse_out, wide, sems):
    first = pltpu.make_async_copy(smooth_in, smooth_out, sems.at[0])
    first.start()
    copies = []
    for i in range(coarse_in.shape[0]):
        wide[i] = coarse_in[i].astype(jnp.float32)
        copy = pltpu.make_async_copy(wide.at[i], coarse_out.at[i], sems.at[1 + i])
        copy.start()
        copies.append(copy)
    first.wait()
    for copy in copies:
        copy.wait()


def widen(smooth, coarse):
    return pl.pallas_call(
        widen_kernel,
        out_shape=(
            jax.ShapeDtypeStruct(smooth.shape, jnp.float32),
            jax.ShapeDtypeStruct(coarse.shape, jnp.float32),
        ),
        in_specs=[pl.BlockSpec(memory_space=pltpu.VMEM)] * 2,
        out_specs=[pl.BlockSpec(memory_space=pltpu.HBM)] * 2,
        scratch_shapes=[pltpu.VMEM(coarse.shape, jnp.float32), pltpu.SemaphoreType.DMA((1 + coarse.shape[0],))],
        compiler_params=pltpu.CompilerParams(vmem_limit_bytes=32 << 20),
    )(smooth, coarse)


def solution(mesh):
    n_row, n_col = mesh.shape["frow"], mesh.shape["fcol"]

    def body(right_side, noise_weight, stencils, neighbours):
        rows, cols, pix = right_side.shape
        slots = stencils.shape[0]
        ext = (rows + 2 * HALO, cols + 2 * SIDE)
        tiles = ext[0] * ext[1]
        listed = jnp.transpose(neighbours, (2, 0, 1))
        smooth, coarse = pl.pallas_call(
            functools.partial(kernel, (n_row, n_col, rows, cols, pix, slots)),
            out_shape=(
                jax.ShapeDtypeStruct((rows, cols, pix), jnp.float32),
                jax.ShapeDtypeStruct((rows // 2, cols // 2 * n_col, pix), jnp.bfloat16),
            ),
            in_specs=[pl.BlockSpec(memory_space=pl.ANY)] * 4,
            out_specs=(pl.BlockSpec(memory_space=pltpu.VMEM), pl.BlockSpec(memory_space=pltpu.VMEM)),
            scratch_shapes=[
                pltpu.VMEM(ext + (pix,), jnp.float32),
                pltpu.VMEM(ext + (pix,), jnp.float32),
                pltpu.VMEM((tiles, pix), jnp.float32),
                pltpu.VMEM((HALO, 3, tiles, pix), jnp.bfloat16),
                pltpu.VMEM((slots, tiles, 128), jnp.bfloat16),
                pltpu.VMEM((pix // 128, rows * ext[1], 128), jnp.float32),
                pltpu.VMEM((slots, rows, cols), jnp.int32),
                pltpu.VMEM((slots, pix, pix), jnp.bfloat16),
                pltpu.VMEM((2 * rows * cols + cols, pix), jnp.bfloat16),
                pltpu.VMEM((2, 2 * HALO * cols + cols, pix), jnp.bfloat16),
                pltpu.VMEM((2, 2 * rows * SIDE + 2 * SIDE, pix), jnp.bfloat16),
                pltpu.VMEM((2, 2 * rows * SIDE + 2 * SIDE, pix), jnp.bfloat16),
                pltpu.VMEM((4, 2 * HALO * SIDE + 2 * SIDE, pix), jnp.bfloat16),
                pltpu.VMEM((6, SIDE, 128), jnp.float32),
                pltpu.SemaphoreType.DMA((4,)),
                pltpu.SemaphoreType.DMA((8,)),
                pltpu.SemaphoreType.DMA((8,)),
                pltpu.SemaphoreType.DMA((65,)),
                pltpu.SemaphoreType.DMA((65,)),
            ],
            compiler_params=pltpu.CompilerParams(
                collective_id=0, has_side_effects=True, vmem_limit_bytes=48 << 20,
            ),
        )(*[pltpu.with_memory_space_constraint(v, pltpu.HBM) for v in (right_side, noise_weight, stencils, listed)])
        return widen(smooth, coarse)

    placed = (P("frow", "fcol", None), P("frow", "fcol", None), P(), P("frow", "fcol", None))
    return jax.shard_map(
        body,
        mesh=mesh,
        in_specs=placed,
        out_specs=(P("frow", "fcol", None), P("frow", None, None)),
        check_vma=False,
    )
```
